32 devices in a mesh: groups: 2 (over x), hour: 16 (over z, y, core).
Axes of the slice: x: 2, y: 2, z: 4, core: 2. Of those that a mesh axis runs over, the one named last changes fastest.
Arguments:
- power: float32 [32, 16, 2048], P('groups', 'hour'), parts along dimension 0, may hold values from -3 to 3
- capacity: float32 [4096], P(('groups', 'hour')), parts along dimension 0, may hold values from 0.01 to 20
- flow_dual: float32 [32, 16, 4096], P('groups', 'hour'), parts along dimension 0, may hold values from -3 to 3
- upper_dual: float32 [32, 16, 2048], P('groups', 'hour'), parts along dimension 0, may hold values from 0 to 0.1
- lower_dual: float32 [32, 16, 2048], P('groups', 'hour'), parts along dimension 0, may hold values from 0 to 0.1
- price: float32 [32, 16], P('groups', 'hour'), parts along dimension 0, may hold values from -5 to 5
- load: bfloat16 [32, 16, 512], P('groups', 'hour'), parts along dimension 0, may hold values from -5 to 5
- shift_factors: bfloat16 [4096, 512], replicated, may hold values from -0.25 to 0.25
- line_limit: float32 [4096], replicated, may hold values from 0.5 to 3
- unit_bus: int32 [2048], replicated, may hold values from 0 to 511
- leakage: float32 [2048], replicated, may hold values from 0.015625 to 0.0625
- initial_state: float32 [4096], P('groups'), parts along dimension 0, may hold values from 0 to 10
- power_limit: float32 [2048], replicated, may hold values from 0.5 to 1.5
- capacity_cost: float32 [2048], replicated, may hold values from 0 to 0.1
Outputs:
- new_power: float32 [32, 16, 2048], P('groups', 'hour'), parts along dimension 0
- new_capacity: float32 [4096], P(('groups', 'hour')), parts along dimension 0
- new_flow_dual: float32 [32, 16, 4096], P('groups', 'hour'), parts along dimension 0
- new_upper_dual: float32 [32, 16, 2048], P('groups', 'hour'), parts along dimension 0
- new_lower_dual: float32 [32, 16, 2048], P('groups', 'hour'), parts along dimension 0
The draws below stay inside these ranges and needn't reach their ends.
There are 2 independent parts, one for each index of `groups`. The reference program is written for one: setup_inputs(seed, part) draws one part's arguments, and reference() takes and returns one part's arrays. A program takes and returns all parts, laid end to end along the dimension named above; an argument that names none is the same for every part. Nothing has to cross between parts.
All inputs are finite; a program needn't handle non-finite values.
Results may differ from the reference program's by a relative error of at most 0.00093.
Values sent between devices are 32-bit elements; how exact they have to be, the bound alone decides.
A program may use at most 128 MiB of HBM per device.

```python
import math
import jax
import jax.numpy as jnp
from jax import lax

U = 2048
LINES = 4096
BUSES = 512
SCEN = 16
ITERS = 4
HOURS = 16


def plant(array, own_key, low, largest):
    index_at = [jax.random.randint(jax.random.fold_in(own_key, axis), (), 0, length) for axis, length in enumerate(array.shape)]
    widest = array.shape.index(max(array.shape))
    neighbour = index_at[:widest] + [(index_at[widest] + 1) % array.shape[widest]] + index_at[widest + 1:]
    return array.at[tuple(index_at)].set(low).at[tuple(neighbour)].set(largest)


def steps_of(key, dims, pieces, smallest, largest):
    loudness, own = 1.0, jax.random.fold_in(key, 6)
    for axis_at, blocks in pieces:
        heights = jnp.exp(jax.random.uniform(jax.random.fold_in(own, axis_at), (blocks,), jnp.float32, smallest / len(pieces), largest / len(pieces)))
        loudness = loudness * jnp.repeat(heights, dims[axis_at] // blocks).reshape([-1 if axis == axis_at else 1 for axis in range(len(dims))])
    return loudness


def gaussian(key, shape, width, reach, cuts=(), kind=jnp.bfloat16):
    result = jax.random.normal(key, shape, jnp.float32) * width
    if len(cuts) > 0:
        result = steps_of(key, shape, cuts, -0.22, 0.18) * result
    return jnp.clip(result, min=-reach, max=reach).astype(kind)


def setup_inputs(seed: int = 0, part: int = 0) -> dict:
    arg_keys = jax.random.split(jax.random.key(seed), 15)
    part_splits = jax.random.split(jax.random.fold_in(arg_keys[14], part), 15)
    return {
        "power": gaussian(part_splits[0], (SCEN, HOURS, U), 0.5, 3.0, ((1, 16),), jnp.float32),
        "capacity": jnp.clip(jnp.exp(math.log(20.0) - 7.6009025 * jax.random.uniform(part_splits[1], (U,), jnp.float32) ** steps_of(part_splits[1], (U,), ((0, 16),), -0.2, 0.2)), 0.01, 20.0),
        "flow_dual": gaussian(part_splits[2], (SCEN, HOURS, LINES), 0.5, 3.0, ((1, 16),), jnp.float32),
        "upper_dual": jnp.clip(0.1 * jax.random.uniform(part_splits[3], (SCEN, HOURS, U), jnp.float32) ** steps_of(part_splits[3], (SCEN, HOURS, U), ((1, 16),), -0.2, 0.2), 0.0, 0.1),
        "lower_dual": jnp.clip(0.1 * jax.random.uniform(part_splits[4], (SCEN, HOURS, U), jnp.float32) ** steps_of(part_splits[4], (SCEN, HOURS, U), ((1, 16),), -0.2, 0.2), 0.0, 0.1),
        "price": gaussian(part_splits[5], (SCEN, HOURS), 1.0, 5.0, ((1, 16),), jnp.float32),
        "load": gaussian(part_splits[6], (SCEN, HOURS, BUSES), 1.0, 5.0, ((1, 16),)),
        "shift_factors": gaussian(arg_keys[7], (LINES, BUSES), BUSES ** -0.5, 0.25),
        "line_limit": jnp.clip(jax.random.uniform(arg_keys[8], (LINES,), jnp.float32, 0.5, 3.0), 0.5, 3.0),
        "unit_bus": plant(jax.random.randint(arg_keys[9], (U,), 0, BUSES), jax.random.fold_in(arg_keys[9], 1), 0, BUSES - 1).astype(jnp.int32),
        "leakage": jnp.clip(jnp.exp(jax.random.uniform(arg_keys[10], (U,), jnp.float32, math.log(0.015625), math.log(0.0625))), 0.015625, 0.0625),
        "initial_state": jnp.clip(jax.random.uniform(part_splits[11], (U,), jnp.float32, 0.0, 10.0), 0.0, 10.0),
        "power_limit": jnp.clip(jax.random.uniform(arg_keys[12], (U,), jnp.float32, 0.5, 1.5), 0.5, 1.5),
        "capacity_cost": jnp.clip(jax.random.uniform(arg_keys[13], (U,), jnp.float32, 0.0, 0.1), 0.0, 0.1),
    }


primal_step = 0.05
dual_step = 0.01


def state_forward(field, retain, start):
    def advance(carry, item):
        carry = retain * carry - item
        return carry, carry
    begin = jnp.broadcast_to(start, (field.shape[0], field.shape[2])).astype(jnp.float32)
    final, states = lax.scan(advance, begin, jnp.moveaxis(field, 1, 0))
    return jnp.moveaxis(states, 0, 1)


def state_adjoint(values, retain):
    def advance(carry, item):
        carry = retain * carry + item
        return carry, carry
    begin = jnp.zeros((values.shape[0], values.shape[2]), jnp.float32)
    final, states = lax.scan(advance, begin, jnp.moveaxis(values, 1, 0), reverse=True)
    return jnp.moveaxis(states, 0, 1)


def reference(power, capacity, flow_dual, upper_dual, lower_dual, price, load, shift_factors, line_limit, unit_bus, leakage, initial_state, power_limit, capacity_cost):
    retain = 1.0 - leakage
    incidence = (unit_bus[:, None] == jnp.arange(BUSES, dtype=jnp.int32)[None, :]).astype(jnp.bfloat16)
    for step in range(ITERS):
        bus_dual = jnp.dot(flow_dual.astype(jnp.bfloat16).reshape(-1, LINES), shift_factors, preferred_element_type=jnp.float32).astype(jnp.bfloat16)
        grid_grad = jnp.dot(bus_dual, incidence.T, preferred_element_type=jnp.float32).reshape(SCEN, HOURS, U)
        state_grad = -state_adjoint(upper_dual - lower_dual, retain)
        trial_power = jnp.clip(power - primal_step * (grid_grad + state_grad - price[:, :, None]), -power_limit, power_limit)
        dual_total = jnp.sum(upper_dual, axis=(0, 1))
        trial_capacity = jnp.maximum(capacity - primal_step * (HOURS * capacity_cost - dual_total / SCEN), 0.0)
        power_bar = 2.0 * trial_power - power
        capacity_bar = 2.0 * trial_capacity - capacity
        injection = jnp.dot(power_bar.astype(jnp.bfloat16).reshape(-1, U), incidence, preferred_element_type=jnp.float32)
        injection = (injection - load.astype(jnp.float32).reshape(-1, BUSES)).astype(jnp.bfloat16)
        flows = jnp.dot(injection, shift_factors.T, preferred_element_type=jnp.float32).reshape(SCEN, HOURS, LINES)
        probe = flow_dual + dual_step * flows
        flow_dual = probe - dual_step * jnp.clip(probe / dual_step, -line_limit, line_limit)
        state_bar = state_forward(power_bar, retain, initial_state)
        upper_dual = jnp.maximum(upper_dual + dual_step * (state_bar - capacity_bar), 0.0)
        lower_dual = jnp.maximum(lower_dual - dual_step * state_bar, 0.0)
        power = trial_power
        capacity = trial_capacity
    return power, capacity, flow_dual, upper_dual, lower_dual
```

```python
import functools

import jax
import jax.numpy as jnp
from jax import lax
from jax.experimental import pallas as pl
from jax.experimental.pallas import tpu as pltpu
from jax.sharding import PartitionSpec as P

ITERS = 4

primal_step = 0.05
dual_step = 0.01


def kernel(n, *refs):
    arrived, refs = refs[:14], refs[14:]
    (power_out, capacity_out, flow_out, upper_out, lower_out), refs = refs[:5], refs[5:]
    held, refs = refs[:14], refs[14:]
    (
        power_in,
        capacity_in,
        flow_in,
        upper_in,
        lower_in,
        price_in,
        load_in,
        shift,
        limit_in,
        bus_in,
        leak_in,
        start_in,
        plimit_in,
        cost_in,
    ) = held
    (
        inc,
        power,
        grid,
        flow,
        bar16,
        upper,
        lower,
        upper_stage,
        lower_stage,
        adj,
        adj_got,
        bar,
        bar_got,
        send_sems,
        recv_sems,
        load_sems,
    ) = refs
    me = lax.axis_index("hour")
    scen, hdev, units = power_in.shape
    lines, buses = shift.shape
    ud = units // n
    hours = hdev * n
    loads = [
        pltpu.make_async_copy(src, dst, load_sems.at[i])
        for i, (src, dst) in enumerate(zip(arrived, held))
    ]
    first = (3, 4)
    for i in first:
        loads[i].start()

    def peer_of(k):
        return me ^ k

    def copy_to(src, dst, channel, peer):
        return pltpu.make_async_remote_copy(
            src_ref=src.at[peer],
            dst_ref=dst.at[me],
            send_sem=send_sems.at[channel, peer],
            recv_sem=recv_sems.at[channel, me],
            device_id={"hour": peer},
            device_id_type=pl.DeviceIdType.MESH,
        )

    def wait_from(dst, channel, source):
        pltpu.make_async_remote_copy(
            src_ref=dst.at[source],
            dst_ref=dst.at[source],
            send_sem=send_sems.at[channel, source],
            recv_sem=recv_sems.at[channel, source],
            device_id={"hour": source},
            device_id_type=pl.DeviceIdType.MESH,
        ).wait_recv()

    blocks = sorted(range(1, n // 4), key=lambda z: -min(z, n // 4 - z))
    order = [z * 4 + low for low in (2, 3, 0, 1) for z in blocks] + [2, 3, 1]
    assert n % 4 == 0 and n & (n - 1) == 0 and sorted(order) == list(range(1, n))

    def each(order, function):
        for k in order:
            function(k)

    def rows_of(ref, lanes):
        return jnp.concatenate([ref[:, j, lanes] for j in range(hdev)], axis=0)

    barrier = pltpu.get_barrier_semaphore()
    each(
        order,
        lambda k: pl.semaphore_signal(
            barrier,
            inc=1,
            device_id={"hour": peer_of(k)},
            device_id_type=pl.DeviceIdType.MESH,
        ),
    )
    for i in (9, 0, 2, 7, 1, 5, 6, 8, 10, 11, 12, 13):
        loads[i].start()
    for i in first:
        loads[i].wait()
    for d in range(n):
        lanes = slice(d * ud, (d + 1) * ud)
        upper_stage[d] = rows_of(upper_in, lanes)
        lower_stage[d] = upper_stage[d] - rows_of(lower_in, lanes)
    pl.semaphore_wait(barrier, n - 1)

    each(order, lambda k: copy_to(lower_stage, lower, 1, peer_of(k)).start())
    each(order, lambda k: copy_to(upper_stage, upper, 0, peer_of(k)).start())
    upper[me] = upper_stage[me]
    lower[me] = lower_stage[me]
    for i in range(14):
        if i not in first and i != 7:
            loads[i].wait()
    for d in range(n):
        power[d] = rows_of(power_in, slice(d * ud, (d + 1) * ud))
    for j in range(hdev):
        flow[j * scen : (j + 1) * scen, :] = flow_in[:, j, :]
    piece = 128
    names = bus_in[...]
    for b in range(0, buses, piece):
        rows = lax.broadcasted_iota(jnp.int32, (piece, units), 0) + b
        inc[b : b + piece, :] = jnp.where(rows == names, 1.0, 0.0).astype(jnp.bfloat16)
    capacity_out[...] = capacity_in[...]
    retain = 1.0 - leak_in[pl.ds(me, 1), :]
    begin = start_in[pl.ds(me, 1), :]
    cost = cost_in[pl.ds(me, 1), :]
    eye = lax.broadcasted_iota(jnp.int32, (scen, scen), 0) == lax.broadcasted_iota(
        jnp.int32, (scen, scen), 1
    )
    price = jnp.concatenate(
        [
            jnp.sum(jnp.where(eye, price_in[j : j + 1, :], 0.0), axis=1, keepdims=True)
            for j in range(hdev)
        ],
        axis=0,
    )
    loads[7].wait()

    def place(t):
        return t // hdev, slice((t % hdev) * scen, (t % hdev + 1) * scen)

    def adjoint(difference):
        w = jnp.zeros((scen, ud), jnp.float32)
        for t in reversed(range(hours)):
            d, rows = place(t)
            w = retain * w + difference(d, rows)
            adj[d, rows, :] = w
        each(order, lambda k: copy_to(adj, adj_got, 2, peer_of(k)).start())
        adj_got[me] = adj[me]

    def iteration(first):
        bus_dual = jnp.dot(
            flow[...].astype(jnp.bfloat16), shift[...], preferred_element_type=jnp.float32
        ).astype(jnp.bfloat16)
        grid_grad = jnp.dot(bus_dual, inc[...], preferred_element_type=jnp.float32)
        for d in range(n):
            grid[d] = grid_grad[:, d * ud : (d + 1) * ud]

        def advance(d):
            limit = plimit_in[pl.ds(d, 1), :]
            old = power[d]
            trial = jnp.clip(
                old - primal_step * (grid[d] - adj_got[d] - price), -limit, limit
            )
            bar[d] = 2.0 * trial - old
            power[d] = trial

        advance(me)
        bar_got[me] = bar[me]

        def answer(k):
            source = peer_of(k)
            wait_from(adj_got, 2, source)
            advance(source)
            copy_to(bar, bar_got, 3, source).start()

        each(order, answer)
        for d in range(n):
            bar16[:, d * ud : (d + 1) * ud] = bar[d].astype(jnp.bfloat16)
        injection = lax.dot_general(
            bar16[...], inc[...], (((1,), (1,)), ((), ())), preferred_element_type=jnp.float32
        )
        load = jnp.concatenate([load_in[j] for j in range(hdev)], axis=0)
        injection = (injection - load.astype(jnp.float32)).astype(jnp.bfloat16)
        width = min(1024, lines)
        for c in range(0, lines, width):
            flows = lax.dot_general(
                injection,
                shift[c : c + width, :],
                (((1,), (1,)), ((), ())),
                preferred_element_type=jnp.float32,
            )
            probe = flow[:, c : c + width] + dual_step * flows
            edge = dual_step * limit_in[:, c : c + width]
            flow[:, c : c + width] = probe - jnp.clip(probe, -edge, edge)

        if first:

            def wait_upper(k):
                wait_from(upper, 0, peer_of(k))
                copy_to(upper_stage, upper, 0, peer_of(k)).wait_send()
                copy_to(lower_stage, lower, 1, peer_of(k)).wait_send()

            each(order, wait_upper)
            for d in range(n):
                lower[d] = upper[d] - lower[d]
        total = jnp.zeros((scen, ud), jnp.float32)
        for t in range(hours):
            d, rows = place(t)
            total = total + upper[d, rows, :]
        dual_total = jnp.sum(total, axis=0, keepdims=True)
        capacity = capacity_out[...]
        trial_capacity = jnp.maximum(
            capacity - primal_step * (hours * cost - dual_total / scen), 0.0
        )
        capacity_bar = 2.0 * trial_capacity - capacity
        capacity_out[...] = trial_capacity

        def wait_bar(k):
            wait_from(bar_got, 3, peer_of(k))
            copy_to(adj, adj_got, 2, peer_of(k)).wait_send()
            copy_to(bar, bar_got, 3, peer_of(k)).wait_send()

        each(order, wait_bar)
        e = jnp.broadcast_to(begin, (scen, ud))
        for t in range(hours):
            d, rows = place(t)
            e = retain * e - bar_got[d, rows, :]
            upper[d, rows, :] = jnp.maximum(
                upper[d, rows, :] + dual_step * (e - capacity_bar), 0.0
            )
            lower[d, rows, :] = jnp.maximum(lower[d, rows, :] - dual_step * e, 0.0)

    each(order, lambda k: wait_from(lower, 1, peer_of(k)))
    adjoint(lambda d, rows: lower[d, rows, :])
    iteration(True)

    def again(step, carry):
        adjoint(lambda d, rows: upper[d, rows, :] - lower[d, rows, :])
        iteration(False)
        return carry

    lax.fori_loop(1, ITERS, again, 0)

    def send_last(k):
        copy_to(upper, adj_got, 2, peer_of(k)).start()
        copy_to(lower, lower_stage, 0, peer_of(k)).start()

    each(order, send_last)
    adj_got[me] = upper[me]
    lower_stage[me] = lower[me]
    for d in range(n):
        for j in range(hdev):
            power_out[:, j, d * ud : (d + 1) * ud] = power[d, j * scen : (j + 1) * scen, :]
    for j in range(hdev):
        flow_out[:, j, :] = flow[j * scen : (j + 1) * scen, :]

    def wait_last(k):
        wait_from(adj_got, 2, peer_of(k))
        wait_from(lower_stage, 0, peer_of(k))
        copy_to(upper, adj_got, 2, peer_of(k)).wait_send()
        copy_to(lower, lower_stage, 0, peer_of(k)).wait_send()

    each(order, wait_last)
    for d in range(n):
        for j in range(hdev):
            lanes, rows = slice(d * ud, (d + 1) * ud), slice(j * scen, (j + 1) * scen)
            upper_out[:, j, lanes] = adj_got[d, rows, :]
            lower_out[:, j, lanes] = lower_stage[d, rows, :]


def store(*refs):
    sems = refs[10]
    copies = [
        pltpu.make_async_copy(refs[i], refs[5 + i], sems.at[i]) for i in (2, 0, 3, 4, 1)
    ]
    for copy in copies:
        copy.start()
    for copy in copies:
        copy.wait()


def kernel_rows(n, *refs):
    hbm, refs = refs[:14], refs[14:]
    (power_out, capacity_out, flow_out, upper_out, lower_out), refs = refs[:5], refs[5:]
    (
        capacity_in,
        flow_home,
        upper_home,
        price_in,
        load_in,
        shift,
        limit_in,
        bus_in,
        leak_in,
        start_in,
        plimit_in,
        cost_in,
        inc,
        upper,
        lower,
        power,
        flow_low,
        flow_high,
        grid,
        bar,
        bar16,
        flow,
        flow2,
        flows1,
        first_src,
        first_dst,
        cap_src,
        cap_dst,
        grad_src,
        grad_dst,
        total_src,
        total_dst,
        part_src,
        part_dst,
        last_src,
        last_dst,
        inj_src,
        inj_dst,
        cap_ref,
        send_sems,
        recv_sems,
        load_sems,
        own_sems,
    ) = refs
    me = lax.axis_index("hour")
    power_hbm, flow_hbm, upper_hbm, lower_hbm = hbm[0], hbm[2], hbm[3], hbm[4]
    hours = scen = n
    lines, buses = shift.shape
    ub, lb, bb = upper_home.shape[1], flow_home.shape[1], buses // 128
    half = lb // 2
    units = ub * 128

    loads = {}

    def load(name, src, dst, i):
        loads[name] = pltpu.make_async_copy(src, dst, load_sems.at[i])
        loads[name].start()

    load("upper", upper_hbm, upper_home, 0)
    load("price", hbm[5], price_in, 1)
    load("flow", flow_hbm, flow_home, 2)
    quarter = lines // 4
    for q in range(4):
        rows = pl.ds(q * quarter, quarter)
        load(("shift", q), hbm[7].at[rows], shift.at[rows], 3 + q)

    blocks = sorted(range(1, n // 4), key=lambda z: -min(z, n // 4 - z))
    order = [z * 4 + low for low in (2, 3, 0, 1) for z in blocks] + [2, 3, 1]
    assert n % 4 == 0 and n & (n - 1) == 0 and sorted(order) == list(range(1, n))

    barrier = pltpu.get_barrier_semaphore()
    for k in order:
        pl.semaphore_signal(
            barrier,
            inc=1,
            device_id={"hour": me ^ k},
            device_id_type=pl.DeviceIdType.MESH,
        )
    for i, (name, src, dst) in enumerate(
        (
            ("load", 6, load_in),
            ("bus", 9, bus_in),
            ("capacity", 1, capacity_in),
            ("cost", 13, cost_in),
            ("leak", 10, leak_in),
            ("plimit", 12, plimit_in),
            ("start", 11, start_in),
            ("limit", 8, limit_in),
        )
    ):
        load(name, hbm[src], dst, 7 + i)
    own = [
        pltpu.make_async_copy(src, dst.at[me], own_sems.at[i])
        for i, (src, dst) in enumerate(
            (
                (upper_hbm.at[me], upper),
                (lower_hbm.at[me], lower),
                (power_hbm.at[me], power),
                (flow_hbm.at[me, pl.ds(0, half)], flow_low),
                (flow_hbm.at[me, pl.ds(half, half)], flow_high),
            )
        )
    ]
    for copy in own:
        copy.start()

    def push(source, dst, channel):
        for k in order:
            peer = me ^ k
            pltpu.make_async_remote_copy(
                src_ref=source(peer),
                dst_ref=dst.at[me],
                send_sem=send_sems.at[channel],
                recv_sem=recv_sems.at[channel],
                device_id={"hour": peer},
                device_id_type=pl.DeviceIdType.MESH,
            ).start()

    def everything(dst, channel):
        rest = dst.at[pl.ds(0, n - 1)]
        return pltpu.make_async_remote_copy(
            src_ref=rest,
            dst_ref=rest,
            send_sem=send_sems.at[channel],
            recv_sem=recv_sems.at[channel],
            device_id={"hour": me ^ 1},
            device_id_type=pl.DeviceIdType.MESH,
        )

    def arrive(dst, channel):
        everything(dst, channel).wait_recv()

    def lanes(j):
        return slice(j * 128, (j + 1) * 128)

    eye = lax.broadcasted_iota(jnp.int32, (scen, scen), 0) == lax.broadcasted_iota(
        jnp.int32, (scen, scen), 1
    )
    loads["upper"].wait()
    loads["price"].wait()
    part = upper_home[0]
    for s in range(1, scen):
        part = part + upper_home[s]
    price = jnp.sum(jnp.where(eye, price_in[...], 0.0), axis=1, keepdims=True)
    first_src[:, 0, :] = part
    first_src[:, 1, :] = jnp.broadcast_to(price, (scen, 128))
    pl.semaphore_wait(barrier, n - 1)

    push(lambda peer: first_src.at[peer], first_dst, 0)
    push(lambda peer: upper_hbm.at[peer], upper, 1)
    push(lambda peer: lower_hbm.at[peer], lower, 2)
    push(lambda peer: power_hbm.at[peer], power, 3)
    first_dst[me] = first_src[me]

    def bus_dual(rows):
        return jnp.dot(
            rows.astype(jnp.bfloat16), shift[...], preferred_element_type=jnp.float32
        ).astype(jnp.bfloat16)

    loads["flow"].wait()
    for j in range(lb):
        flow2[:, lanes(j)] = flow_home[:, j, :]
    for q in range(4):
        loads[("shift", q)].wait()
    dual = bus_dual(flow2[...]).astype(jnp.float32)
    loads["load"].wait()
    demand = load_in[0].astype(jnp.float32)
    for j in range(bb):
        grad_src[:, j, :] = dual[:, lanes(j)]
        grad_src[:, bb + j, :] = demand[:, lanes(j)]
    push(lambda peer: grad_src.at[peer], grad_dst, 4)
    grad_dst[me] = grad_src[me]

    loads["capacity"].wait()
    loads["cost"].wait()
    arrive(first_dst, 0)
    my_cost = cost_in[pl.ds(me, 1), :]

    def next_capacity(old, cost, total):
        return jnp.maximum(old - primal_step * (hours * cost - total / scen), 0.0)

    old = capacity_in[...]
    trial = next_capacity(old, my_cost, jnp.sum(first_dst[:, 0, :], axis=0, keepdims=True))
    cap_src[0:1, :] = trial
    cap_src[1:2, :] = 2.0 * trial - old
    push(lambda peer: cap_src, cap_dst, 5)
    cap_dst[me] = cap_src[...]
    push(lambda peer: flow_hbm.at[peer, pl.ds(0, half)], flow_low, 6)
    push(lambda peer: flow_hbm.at[peer, pl.ds(half, half)], flow_high, 7)

    for name in ("bus", "leak", "plimit", "start", "limit"):
        loads[name].wait()
    piece = 128
    names = bus_in[...]
    for b in range(0, buses, piece):
        rows = lax.broadcasted_iota(jnp.int32, (piece, units), 0) + b
        inc[b : b + piece, :] = jnp.where(rows == names, 1.0, 0.0).astype(jnp.bfloat16)
    retain = 1.0 - leak_in[...]
    plimit = plimit_in[...]
    width = min(1024, lines)

    def gradient(dual):
        value = jnp.dot(dual, inc[...], preferred_element_type=jnp.float32)
        for j in range(ub):
            grid[:, j, :] = value[:, lanes(j)]

    def primal():
        w = jnp.zeros((ub, 128), jnp.float32)
        for t in reversed(range(hours)):
            w = retain * w + (upper[t] - lower[t])
            old = power[t]
            trial = jnp.clip(
                old - primal_step * (grid[t] - w - first_dst[t, 1:2, :]), -plimit, plimit
            )
            bar[t] = 2.0 * trial - old
            power[t] = trial

    def states(function):
        e = start_in[...]
        for t in range(hours):
            e = retain * e - bar[t]
            function(t, e)

    def inject(i):
        for j in range(ub):
            bar16[:, lanes(j)] = bar[:, j, :].astype(jnp.bfloat16)
        value = lax.dot_general(
            bar16[...], inc[...], (((1,), (1,)), ((), ())), preferred_element_type=jnp.float32
        )
        demand = jnp.concatenate([grad_dst[:, bb + j, :] for j in range(bb)], axis=1)
        value = (value - demand).astype(jnp.bfloat16)
        wide = value.astype(jnp.float32)
        for j in range(bb):
            inj_src[i, :, j, :] = wide[:, lanes(j)]
        push(lambda peer: inj_src.at[i, peer], inj_dst.at[i], 8 + i)
        inj_dst[i, me] = inj_src[i, me]
        return value

    def injected(i):
        arrive(inj_dst.at[i], 8 + i)
        return jnp.concatenate([inj_dst[i, :, j, :] for j in range(bb)], axis=1).astype(
            jnp.bfloat16
        )

    def line_flows(value, c):
        return lax.dot_general(
            value,
            shift[c : c + width, :],
            (((1,), (1,)), ((), ())),
            preferred_element_type=jnp.float32,
        )

    def advance(ref, c, flows):
        probe = ref[:, c : c + width] + dual_step * flows
        edge = dual_step * limit_in[:, c : c + width]
        ref[:, c : c + width] = probe - jnp.clip(probe, -edge, edge)

    def update_duals(capacity_bar):
        totals = [jnp.zeros((ub, 128), jnp.float32)]

        def update(t, e):
            raised = jnp.maximum(upper[t] + dual_step * (e - capacity_bar), 0.0)
            upper[t] = raised
            totals[0] = totals[0] + raised
            lower[t] = jnp.maximum(lower[t] - dual_step * e, 0.0)

        states(update)
        return totals[0]

    def broadcast(i, total):
        total_src[i] = total
        push(lambda peer: total_src.at[i], total_dst.at[i], 12 + i)
        total_dst[i, me] = total

    def capacity_step(i):
        arrive(total_dst.at[i], 12 + i)
        total = total_dst[i, 0]
        for d in range(1, n):
            total = total + total_dst[i, d]
        old = cap_ref[...]
        trial = next_capacity(old, cost_in[...], total)
        cap_ref[...] = trial
        return 2.0 * trial - old

    for copy in own:
        copy.wait()
    arrive(grad_dst, 4)
    gradient(
        jnp.concatenate([grad_dst[:, j, :] for j in range(bb)], axis=1).astype(jnp.bfloat16)
    )
    arrive(upper, 1)
    arrive(lower, 2)
    arrive(power, 3)
    primal()
    arrive(cap_dst, 5)
    cap_ref[...] = cap_dst[:, 0, :]
    broadcast(0, update_duals(cap_dst[:, 1, :]))
    value = inject(0)
    for c in range(0, lines, width):
        flows1[:, c : c + width] = line_flows(value, c)
    for part, ref, channel in ((0, flow_low, 6), (1, flow_high, 7)):
        arrive(ref, channel)
        for j in range(half):
            flow[:, lanes(part * half + j)] = ref[:, j, :]
    for c in range(0, lines, width):
        advance(flow, c, flows1[:, c : c + width])

    for step in (1, 2):
        gradient(bus_dual(flow[...]))
        primal()
        total = update_duals(capacity_step(step - 1))
        if step == 1:
            broadcast(1, total)
        else:
            part_src[:, 0, :] = total
            push(lambda peer: part_src.at[peer], part_dst, 14)
            part_dst[me] = part_src[me]
        value = inject(step)
        both = jnp.concatenate([value, injected(step - 1)], axis=0)
        for c in range(0, lines, width):
            flows = line_flows(both, c)
            advance(flow, c, flows[:n])
            advance(flow2, c, flows[n:])

    gradient(bus_dual(flow[...]))
    primal()
    push(lambda peer: power.at[peer], power_out, 15)
    power_out[me] = power[me]
    inject(3)

    def last(t, e):
        upper[t] = upper[t] + dual_step * e
        lower[t] = jnp.maximum(lower[t] - dual_step * e, 0.0)

    states(last)
    push(lambda peer: lower.at[peer], lower_out, 16)
    push(lambda peer: upper.at[peer], upper_out, 17)
    lower_out[me] = lower[me]
    upper_out[me] = upper[me]
    arrive(part_dst, 14)
    old = cap_ref[pl.ds(me, 1), :]
    trial = next_capacity(old, my_cost, jnp.sum(part_dst[:, 0, :], axis=0, keepdims=True))
    capacity_out[...] = trial
    last_src[...] = 2.0 * trial - old
    push(lambda peer: last_src, last_dst, 18)
    last_dst[me] = last_src[...]

    for i in (2, 3):
        value = injected(i)
        for c in range(0, lines, width):
            advance(flow2, c, line_flows(value, c))
    for j in range(lb):
        flow_out[:, j, :] = flow2[:, lanes(j)]
    arrive(power_out, 15)
    arrive(lower_out, 16)
    arrive(last_dst, 18)
    raised = dual_step * last_dst[:, 0, :]
    arrive(upper_out, 17)
    for s in range(scen):
        upper_out[s] = jnp.maximum(upper_out[s] - raised, 0.0)
    sent = (
        [first_dst, upper, lower, power, grad_dst, cap_dst, flow_low, flow_high]
        + [inj_dst.at[i] for i in range(4)]
        + [total_dst.at[i] for i in range(2)]
        + [part_dst, power_out, lower_out, upper_out, last_dst]
    )
    for channel, dst in enumerate(sent):
        everything(dst, channel).wait_send()


def by_rows(n, args):
    power, capacity, flow, upper, lower, price, load, shift, limit, bus = args[:10]
    leak, start, plimit, cost = args[10:]
    scen, _, units = power.shape
    lines, buses = shift.shape
    ub, lb, bb = units // 128, lines // 128, buses // 128
    vmem = pl.BlockSpec(memory_space=pltpu.VMEM)
    hbm = pl.BlockSpec(memory_space=pltpu.HBM)
    state, wide = (scen, ub, 128), (scen, lb, 128)
    args = (
        power.reshape(state),
        capacity,
        flow.reshape(wide),
        upper.reshape(state),
        lower.reshape(state),
        price,
        load,
        shift,
        limit,
        bus,
        leak,
        start,
        plimit,
        cost,
    )
    f32 = jnp.float32
    results = tuple(jax.ShapeDtypeStruct(args[i].shape, f32) for i in range(5))

    def buffer(*shape, dtype=f32):
        return pltpu.VMEM(shape, dtype)

    out = pl.pallas_call(
        functools.partial(kernel_rows, n),
        out_shape=results,
        in_specs=[hbm] * 14,
        out_specs=(vmem,) * 5,
        scratch_shapes=[pltpu.VMEM(args[i].shape, args[i].dtype) for i in (1, 2, 3)]
        + [pltpu.VMEM(a.shape, a.dtype) for a in args[5:]]
        + [buffer(buses, units, dtype=jnp.bfloat16)]
        + [buffer(*state)] * 3
        + [buffer(n, lb // 2, 128)] * 2
        + [buffer(*state)] * 2
        + [buffer(n, units, dtype=jnp.bfloat16)]
        + [buffer(n, lines)] * 3
        + [
            buffer(n, 2, 128),
            buffer(n, 2, 128),
            buffer(2, 128),
            buffer(n, 2, 128),
            buffer(n, 2 * bb, 128),
            buffer(n, 2 * bb, 128),
            buffer(2, ub, 128),
            buffer(2, n, ub, 128),
            buffer(n, 1, 128),
            buffer(n, 1, 128),
            buffer(1, 128),
            buffer(n, 1, 128),
            buffer(4, n, bb, 128),
            buffer(4, n, bb, 128),
            buffer(ub, 128),
            pltpu.SemaphoreType.DMA((19,)),
            pltpu.SemaphoreType.DMA((19,)),
            pltpu.SemaphoreType.DMA((15,)),
            pltpu.SemaphoreType.DMA((5,)),
        ],
        compiler_params=pltpu.CompilerParams(
            collective_id=0, has_side_effects=True, vmem_limit_bytes=48 * 1024 * 1024
        ),
    )(*(pltpu.with_memory_space_constraint(a, pltpu.HBM) for a in args))
    out = pl.pallas_call(
        store,
        out_shape=results,
        in_specs=[vmem] * 5,
        out_specs=(hbm,) * 5,
        scratch_shapes=[pltpu.SemaphoreType.DMA((5,))],
        compiler_params=pltpu.CompilerParams(vmem_limit_bytes=16 * 1024 * 1024),
    )(*out)
    return (
        out[0].reshape(power.shape),
        out[1].reshape(units // n),
        out[2].reshape(flow.shape),
        out[3].reshape(upper.shape),
        out[4].reshape(lower.shape),
    )


def on_device(
    power,
    capacity,
    flow_dual,
    upper_dual,
    lower_dual,
    price,
    load,
    shift_factors,
    line_limit,
    unit_bus,
    leakage,
    initial_state,
    power_limit,
    capacity_cost,
):
    n = lax.axis_size("hour")
    scen, hdev, units = power.shape
    lines, buses = shift_factors.shape
    ud, rows = units // n, scen * hdev
    block = pltpu.VMEM((n, rows, ud), jnp.float32)
    vmem = pl.BlockSpec(memory_space=pltpu.VMEM)
    hbm = pl.BlockSpec(memory_space=pltpu.HBM)
    args = (
        power,
        capacity.reshape(1, ud),
        flow_dual,
        upper_dual,
        lower_dual,
        price.T,
        load.transpose(1, 0, 2),
        shift_factors,
        line_limit.reshape(1, lines),
        unit_bus.reshape(1, units),
        leakage.reshape(n, ud),
        initial_state.reshape(n, ud),
        power_limit.reshape(n, ud),
        capacity_cost.reshape(n, ud),
    )
    if scen == n and hdev == 1 and ud == 128 and lines % 1024 == 0 and buses % 128 == 0:
        return by_rows(n, args)
    results = tuple(
        jax.ShapeDtypeStruct(args[i].shape, jnp.float32) for i in range(5)
    )
    out = pl.pallas_call(
        functools.partial(kernel, n),
        out_shape=results,
        in_specs=[hbm] * 14,
        out_specs=(vmem,) * 5,
        scratch_shapes=[pltpu.VMEM(a.shape, a.dtype) for a in args]
        + [
            pltpu.VMEM((buses, units), jnp.bfloat16),
            block,
            block,
            pltpu.VMEM((rows, lines), jnp.float32),
            pltpu.VMEM((rows, units), jnp.bfloat16),
        ]
        + [block] * 8
        + [
            pltpu.SemaphoreType.DMA((4, n)),
            pltpu.SemaphoreType.DMA((4, n)),
            pltpu.SemaphoreType.DMA((14,)),
        ],
        compiler_params=pltpu.CompilerParams(
            collective_id=0, has_side_effects=True, vmem_limit_bytes=48 * 1024 * 1024
        ),
    )(*(pltpu.with_memory_space_constraint(a, pltpu.HBM) for a in args))
    out = pl.pallas_call(
        store,
        out_shape=results,
        in_specs=[vmem] * 5,
        out_specs=(hbm,) * 5,
        scratch_shapes=[pltpu.SemaphoreType.DMA((5,))],
        compiler_params=pltpu.CompilerParams(vmem_limit_bytes=16 * 1024 * 1024),
    )(*out)
    return (out[0], out[1].reshape(ud), out[2], out[3], out[4])


def solution(mesh):
    return jax.shard_map(
        on_device,
        mesh=mesh,
        in_specs=(
            P("groups", "hour", None),
            P(("groups", "hour")),
            P("groups", "hour", None),
            P("groups", "hour", None),
            P("groups", "hour", None),
            P("groups", "hour"),
            P("groups", "hour", None),
            P(),
            P(),
            P(),
            P(),
            P("groups"),
            P(),
            P(),
        ),
        out_specs=(
            P("groups", "hour", None),
            P(("groups", "hour")),
            P("groups", "hour", None),
            P("groups", "hour", None),
            P("groups", "hour", None),
        ),
        check_vma=False,
    )
```

```python
import functools

import jax
import jax.numpy as jnp
from jax import lax
from jax.experimental import pallas as pl
from jax.experimental.pallas import tpu as pltpu
from jax.sharding import PartitionSpec as P

ITERS = 4

primal_step = 0.05
dual_step = 0.01


def kernel(n, *refs):
    arrived, refs = refs[:14], refs[14:]
    (power_out, capacity_out, flow_out, upper_out, lower_out), refs = refs[:5], refs[5:]
    held, refs = refs[:14], refs[14:]
    (
        power_in,
        capacity_in,
        flow_in,
        upper_in,
        lower_in,
        price_in,
        load_in,
        shift,
        limit_in,
        bus_in,
        leak_in,
        start_in,
        plimit_in,
        cost_in,
    ) = held
    (
        inc,
        power,
        grid,
        flow,
        bar16,
        upper,
        lower,
        upper_stage,
        lower_stage,
        adj,
        adj_got,
        bar,
        bar_got,
        send_sems,
        recv_sems,
        load_sems,
    ) = refs
    me = lax.axis_index("hour")
    scen, hdev, units = power_in.shape
    lines, buses = shift.shape
    ud = units // n
    hours = hdev * n
    loads = [
        pltpu.make_async_copy(src, dst, load_sems.at[i])
        for i, (src, dst) in enumerate(zip(arrived, held))
    ]
    first = (3, 4)
    for i in first:
        loads[i].start()

    def peer_of(k):
        return me ^ k

    def copy_to(src, dst, channel, peer):
        return pltpu.make_async_remote_copy(
            src_ref=src.at[peer],
            dst_ref=dst.at[me],
            send_sem=send_sems.at[channel, peer],
            recv_sem=recv_sems.at[channel, me],
            device_id={"hour": peer},
            device_id_type=pl.DeviceIdType.MESH,
        )

    def wait_from(dst, channel, source):
        pltpu.make_async_remote_copy(
            src_ref=dst.at[source],
            dst_ref=dst.at[source],
            send_sem=send_sems.at[channel, source],
            recv_sem=recv_sems.at[channel, source],
            device_id={"hour": source},
            device_id_type=pl.DeviceIdType.MESH,
        ).wait_recv()

    blocks = sorted(range(1, n // 4), key=lambda z: -min(z, n // 4 - z))
    order = [z * 4 + low for low in (2, 3, 0, 1) for z in blocks] + [2, 3, 1]
    assert n % 4 == 0 and n & (n - 1) == 0 and sorted(order) == list(range(1, n))

    def each(order, function):
        for k in order:
            function(k)

    def rows_of(ref, lanes):
        return jnp.concatenate([ref[:, j, lanes] for j in range(hdev)], axis=0)

    barrier = pltpu.get_barrier_semaphore()
    each(
        order,
        lambda k: pl.semaphore_signal(
            barrier,
            inc=1,
            device_id={"hour": peer_of(k)},
            device_id_type=pl.DeviceIdType.MESH,
        ),
    )
    for i in (9, 0, 2, 7, 1, 5, 6, 8, 10, 11, 12, 13):
        loads[i].start()
    for i in first:
        loads[i].wait()
    for d in range(n):
        lanes = slice(d * ud, (d + 1) * ud)
        upper_stage[d] = rows_of(upper_in, lanes)
        lower_stage[d] = upper_stage[d] - rows_of(lower_in, lanes)
    pl.semaphore_wait(barrier, n - 1)

    each(order, lambda k: copy_to(lower_stage, lower, 1, peer_of(k)).start())
    each(order, lambda k: copy_to(upper_stage, upper, 0, peer_of(k)).start())
    upper[me] = upper_stage[me]
    lower[me] = lower_stage[me]
    for i in range(14):
        if i not in first and i != 7:
            loads[i].wait()
    for d in range(n):
        power[d] = rows_of(power_in, slice(d * ud, (d + 1) * ud))
    for j in range(hdev):
        flow[j * scen : (j + 1) * scen, :] = flow_in[:, j, :]
    piece = 128
    names = bus_in[...]
    for b in range(0, buses, piece):
        rows = lax.broadcasted_iota(jnp.int32, (piece, units), 0) + b
        inc[b : b + piece, :] = jnp.where(rows == names, 1.0, 0.0).astype(jnp.bfloat16)
    capacity_out[...] = capacity_in[...]
    retain = 1.0 - leak_in[pl.ds(me, 1), :]
    begin = start_in[pl.ds(me, 1), :]
    cost = cost_in[pl.ds(me, 1), :]
    eye = lax.broadcasted_iota(jnp.int32, (scen, scen), 0) == lax.broadcasted_iota(
        jnp.int32, (scen, scen), 1
    )
    price = jnp.concatenate(
        [
            jnp.sum(jnp.where(eye, price_in[j : j + 1, :], 0.0), axis=1, keepdims=True)
            for j in range(hdev)
        ],
        axis=0,
    )
    loads[7].wait()

    def place(t):
        return t // hdev, slice((t % hdev) * scen, (t % hdev + 1) * scen)

    def adjoint(difference):
        w = jnp.zeros((scen, ud), jnp.float32)
        for t in reversed(range(hours)):
            d, rows = place(t)
            w = retain * w + difference(d, rows)
            adj[d, rows, :] = w
        each(order, lambda k: copy_to(adj, adj_got, 2, peer_of(k)).start())
        adj_got[me] = adj[me]

    def iteration(first):
        bus_dual = jnp.dot(
            flow[...].astype(jnp.bfloat16), shift[...], preferred_element_type=jnp.float32
        ).astype(jnp.bfloat16)
        grid_grad = jnp.dot(bus_dual, inc[...], preferred_element_type=jnp.float32)
        for d in range(n):
            grid[d] = grid_grad[:, d * ud : (d + 1) * ud]

        def advance(d):
            limit = plimit_in[pl.ds(d, 1), :]
            old = power[d]
            trial = jnp.clip(
                old - primal_step * (grid[d] - adj_got[d] - price), -limit, limit
            )
            bar[d] = 2.0 * trial - old
            power[d] = trial

        advance(me)
        bar_got[me] = bar[me]

        def answer(k):
            source = peer_of(k)
            wait_from(adj_got, 2, source)
            advance(source)
            copy_to(bar, bar_got, 3, source).start()

        each(order, answer)
        for d in range(n):
            bar16[:, d * ud : (d + 1) * ud] = bar[d].astype(jnp.bfloat16)
        injection = lax.dot_general(
            bar16[...], inc[...], (((1,), (1,)), ((), ())), preferred_element_type=jnp.float32
        )
        load = jnp.concatenate([load_in[j] for j in range(hdev)], axis=0)
        injection = (injection - load.astype(jnp.float32)).astype(jnp.bfloat16)
        width = min(1024, lines)
        for c in range(0, lines, width):
            flows = lax.dot_general(
                injection,
                shift[c : c + width, :],
                (((1,), (1,)), ((), ())),
                preferred_element_type=jnp.float32,
            )
            probe = flow[:, c : c + width] + dual_step * flows
            edge = dual_step * limit_in[:, c : c + width]
            flow[:, c : c + width] = probe - jnp.clip(probe, -edge, edge)

        if first:

            def wait_upper(k):
                wait_from(upper, 0, peer_of(k))
                copy_to(upper_stage, upper, 0, peer_of(k)).wait_send()
                copy_to(lower_stage, lower, 1, peer_of(k)).wait_send()

            each(order, wait_upper)
            for d in range(n):
                lower[d] = upper[d] - lower[d]
        total = jnp.zeros((scen, ud), jnp.float32)
        for t in range(hours):
            d, rows = place(t)
            total = total + upper[d, rows, :]
        dual_total = jnp.sum(total, axis=0, keepdims=True)
        capacity = capacity_out[...]
        trial_capacity = jnp.maximum(
            capacity - primal_step * (hours * cost - dual_total / scen), 0.0
        )
        capacity_bar = 2.0 * trial_capacity - capacity
        capacity_out[...] = trial_capacity

        def wait_bar(k):
            wait_from(bar_got, 3, peer_of(k))
            copy_to(adj, adj_got, 2, peer_of(k)).wait_send()
            copy_to(bar, bar_got, 3, peer_of(k)).wait_send()

        each(order, wait_bar)
        e = jnp.broadcast_to(begin, (scen, ud))
        for t in range(hours):
            d, rows = place(t)
            e = retain * e - bar_got[d, rows, :]
            upper[d, rows, :] = jnp.maximum(
                upper[d, rows, :] + dual_step * (e - capacity_bar), 0.0
            )
            lower[d, rows, :] = jnp.maximum(lower[d, rows, :] - dual_step * e, 0.0)

    each(order, lambda k: wait_from(lower, 1, peer_of(k)))
    adjoint(lambda d, rows: lower[d, rows, :])
    iteration(True)

    def again(step, carry):
        adjoint(lambda d, rows: upper[d, rows, :] - lower[d, rows, :])
        iteration(False)
        return carry

    lax.fori_loop(1, ITERS, again, 0)

    def send_last(k):
        copy_to(upper, adj_got, 2, peer_of(k)).start()
        copy_to(lower, lower_stage, 0, peer_of(k)).start()

    each(order, send_last)
    adj_got[me] = upper[me]
    lower_stage[me] = lower[me]
    for d in range(n):
        for j in range(hdev):
            power_out[:, j, d * ud : (d + 1) * ud] = power[d, j * scen : (j + 1) * scen, :]
    for j in range(hdev):
        flow_out[:, j, :] = flow[j * scen : (j + 1) * scen, :]

    def wait_last(k):
        wait_from(adj_got, 2, peer_of(k))
        wait_from(lower_stage, 0, peer_of(k))
        copy_to(upper, adj_got, 2, peer_of(k)).wait_send()
        copy_to(lower, lower_stage, 0, peer_of(k)).wait_send()

    each(order, wait_last)
    for d in range(n):
        for j in range(hdev):
            lanes, rows = slice(d * ud, (d + 1) * ud), slice(j * scen, (j + 1) * scen)
            upper_out[:, j, lanes] = adj_got[d, rows, :]
            lower_out[:, j, lanes] = lower_stage[d, rows, :]


def store(*refs):
    sems = refs[10]
    copies = [
        pltpu.make_async_copy(refs[i], refs[5 + i], sems.at[i]) for i in (2, 0, 3, 4, 1)
    ]
    for copy in copies:
        copy.start()
    for copy in copies:
        copy.wait()


def kernel_rows(n, *refs):
    hbm, refs = refs[:14], refs[14:]
    (power_out, capacity_out, flow_out, upper_out, lower_out), refs = refs[:5], refs[5:]
    (
        capacity_in,
        flow_home,
        upper_home,
        price_in,
        load_in,
        shift,
        limit_in,
        bus_in,
        leak_in,
        start_in,
        plimit_in,
        cost_in,
        inc,
        inc_t,
        shift_t,
        upper,
        lower,
        power,
        flow_in,
        grid,
        bar,
        bar16,
        flow,
        flow2,
        flows1,
        first_src,
        first_dst,
        cap_src,
        cap_dst,
        grad_src,
        grad_dst,
        total_src,
        pair_dst,
        chip_src,
        total_dst,
        part_src,
        part_dst,
        last_src,
        last_dst,
        inj_src,
        inj_dst,
        state,
        power_home,
        adjoint,
        adjoint_home,
        cap_ref,
        send_sems,
        recv_sems,
        pair_send,
        pair_recv,
        load_sems,
        own_sems,
    ) = refs
    me = lax.axis_index("hour")
    power_hbm, flow_hbm, upper_hbm, lower_hbm = hbm[0], hbm[2], hbm[3], hbm[4]
    hours = scen = n
    lines, buses = shift.shape
    ub, lb, bb = upper_home.shape[1], flow_home.shape[1], buses // 128
    quarter_lb = lb // 4
    units = ub * 128

    blocks = sorted(range(1, n // 4), key=lambda z: -min(z, n // 4 - z))
    order = [z * 4 + low for low in (2, 3, 0, 1) for z in blocks] + [2, 3, 1]
    assert n % 4 == 0 and n & (n - 1) == 0 and sorted(order) == list(range(1, n))

    barrier = pltpu.get_barrier_semaphore()
    for k in order:
        pl.semaphore_signal(
            barrier,
            inc=1,
            device_id={"hour": me ^ k},
            device_id_type=pl.DeviceIdType.MESH,
        )
    loads = {}

    def load(name, src, dst, i):
        loads[name] = pltpu.make_async_copy(src, dst, load_sems.at[i])
        loads[name].start()

    load("upper", upper_hbm, upper_home, 0)
    load("price", hbm[5], price_in, 1)
    load("flow", flow_hbm, flow_home, 2)
    quarter = lines // 4
    for q in range(4):
        rows = pl.ds(q * quarter, quarter)
        load(("shift", q), hbm[7].at[rows], shift.at[rows], 3 + q)

    for i, (name, src, dst) in enumerate(
        (
            ("load", 6, load_in),
            ("bus", 9, bus_in),
            ("capacity", 1, capacity_in),
            ("cost", 13, cost_in),
            ("leak", 10, leak_in),
            ("plimit", 12, plimit_in),
            ("start", 11, start_in),
            ("limit", 8, limit_in),
        )
    ):
        load(name, hbm[src], dst, 7 + i)
    own = [
        pltpu.make_async_copy(src, dst.at[me], own_sems.at[i])
        for i, (src, dst) in enumerate(
            (
                (upper_hbm.at[me], upper),
                (lower_hbm.at[me], lower),
                (power_hbm.at[me], power),
            )
            + tuple(
                (flow_hbm.at[me, pl.ds(q * quarter_lb, quarter_lb)], flow_in.at[q])
                for q in range(4)
            )
        )
    ]
    for copy in own:
        copy.start()

    def push(source, dst, channel):
        for k in order:
            peer = me ^ k
            pltpu.make_async_remote_copy(
                src_ref=source(peer),
                dst_ref=dst.at[me],
                send_sem=send_sems.at[channel],
                recv_sem=recv_sems.at[channel],
                device_id={"hour": peer},
                device_id_type=pl.DeviceIdType.MESH,
            ).start()

    def everything(dst, channel):
        rest = dst.at[pl.ds(0, n - 1)]
        return pltpu.make_async_remote_copy(
            src_ref=rest,
            dst_ref=rest,
            send_sem=send_sems.at[channel],
            recv_sem=recv_sems.at[channel],
            device_id={"hour": me ^ 1},
            device_id_type=pl.DeviceIdType.MESH,
        )

    def arrive(dst, channel):
        everything(dst, channel).wait_recv()

    def lanes(j):
        return slice(j * 128, (j + 1) * 128)

    eye = lax.broadcasted_iota(jnp.int32, (scen, scen), 0) == lax.broadcasted_iota(
        jnp.int32, (scen, scen), 1
    )
    loads["upper"].wait()
    loads["price"].wait()
    part = upper_home[0]
    for s in range(1, scen):
        part = part + upper_home[s]
    price = jnp.sum(jnp.where(eye, price_in[...], 0.0), axis=1, keepdims=True)
    first_src[:, 0, :] = part
    first_src[:, 1, :] = jnp.broadcast_to(price, (scen, 128))
    pl.semaphore_wait(barrier, n - 1)

    push(lambda peer: first_src.at[peer], first_dst, 0)
    push(lambda peer: upper_hbm.at[peer], upper, 1)
    first_dst[me] = first_src[me]

    def bus_dual(rows):
        return jnp.dot(
            rows.astype(jnp.bfloat16), shift[...], preferred_element_type=jnp.float32
        ).astype(jnp.bfloat16)

    loads["flow"].wait()
    for j in range(lb):
        flow2[:, lanes(j)] = flow_home[:, j, :]
    for q in range(4):
        loads[("shift", q)].wait()
    dual = bus_dual(flow2[...]).astype(jnp.float32)
    loads["load"].wait()
    demand = load_in[0].astype(jnp.float32)
    for j in range(bb):
        grad_src[:, j, :] = dual[:, lanes(j)]
        grad_src[:, bb + j, :] = demand[:, lanes(j)]
    push(lambda peer: grad_src.at[peer], grad_dst, 4)
    grad_dst[me] = grad_src[me]

    loads["capacity"].wait()
    loads["cost"].wait()
    arrive(first_dst, 0)
    my_cost = cost_in[pl.ds(me, 1), :]

    def next_capacity(old, cost, total):
        return jnp.maximum(old - primal_step * (hours * cost - total / scen), 0.0)

    old = capacity_in[...]
    trial = next_capacity(old, my_cost, jnp.sum(first_dst[:, 0, :], axis=0, keepdims=True))
    cap_src[0:1, :] = trial
    cap_src[1:2, :] = 2.0 * trial - old
    push(lambda peer: cap_src, cap_dst, 5)
    cap_dst[me] = cap_src[...]
    push(lambda peer: lower_hbm.at[peer], lower, 2)
    push(lambda peer: power_hbm.at[peer], power, 3)

    for name in ("bus", "leak", "plimit", "start", "limit"):
        loads[name].wait()
    piece = 128
    names = bus_in[...]
    for b in range(0, buses, piece):
        rows = lax.broadcasted_iota(jnp.int32, (piece, units), 0) + b
        inc[b : b + piece, :] = jnp.where(rows == names, 1.0, 0.0).astype(jnp.bfloat16)
    retain = 1.0 - leak_in[...]
    plimit = plimit_in[...]
    for b in range(0, buses, piece):
        inc_t[:, b : b + piece] = inc[b : b + piece, :].T
    for c in range(0, lines, 512):
        shift_t[:, c : c + 512] = shift[c : c + 512, :].T
    width = min(1024, lines)

    def gradient(dual):
        value = jnp.dot(dual, inc[...], preferred_element_type=jnp.float32)
        for j in range(ub):
            grid[:, j, :] = value[:, lanes(j)]

    def adjoints():
        w = jnp.zeros((ub, 128), jnp.float32)
        for t in reversed(range(hours)):
            w = retain * w + (upper[t] - lower[t])
            adjoint[t] = w

    def primal(old_from, dual_from, prices, new_to):
        for t in range(hours):
            old = old_from[t]
            trial = jnp.clip(
                old - primal_step * (grid[t] - dual_from[t] - prices[t, 1:2, :]),
                -plimit,
                plimit,
            )
            bar[t] = 2.0 * trial - old
            if new_to is not None:
                new_to[t] = trial

    def states():
        e = start_in[...]
        for t in range(hours):
            e = retain * e - bar[t]
            state[t] = e

    def injection(demand_from):
        for j in range(ub):
            bar16[:, lanes(j)] = bar[:, j, :].astype(jnp.bfloat16)
        value = jnp.dot(bar16[...], inc_t[...], preferred_element_type=jnp.float32)
        demand = jnp.concatenate([demand_from[:, bb + j, :] for j in range(bb)], axis=1)
        return (value - demand).astype(jnp.bfloat16)

    def inject(i):
        value = injection(grad_dst)
        wide = value.astype(jnp.float32)
        for j in range(bb):
            inj_src[i, :, j, :] = wide[:, lanes(j)]
        return value

    def send_injection(i):
        push(lambda peer: inj_src.at[i, peer], inj_dst.at[i], 8 + i)
        inj_dst[i, me] = inj_src[i, me]

    def injected(i):
        arrive(inj_dst.at[i], 8 + i)
        return jnp.concatenate([inj_dst[i, :, j, :] for j in range(bb)], axis=1).astype(
            jnp.bfloat16
        )

    def line_flows(value, c):
        return jnp.dot(value, shift_t[:, c : c + width], preferred_element_type=jnp.float32)

    def advance(ref, c, flows):
        probe = ref[:, c : c + width] + dual_step * flows
        edge = dual_step * limit_in[:, c : c + width]
        ref[:, c : c + width] = probe - jnp.clip(probe, -edge, edge)

    def lines_step(ref, value):
        for c in range(0, lines, width):
            advance(ref, c, line_flows(value, c))

    def update_duals(capacity_bar):
        total = jnp.zeros((ub, 128), jnp.float32)
        for t in range(hours):
            e = state[t]
            raised = jnp.maximum(upper[t] + dual_step * (e - capacity_bar), 0.0)
            upper[t] = raised
            total = total + raised
            lower[t] = jnp.maximum(lower[t] - dual_step * e, 0.0)
        return total

    hb = ub // 2
    side = me % 2

    def pair_copy(i):
        return pltpu.make_async_remote_copy(
            src_ref=total_src.at[i, 1 - side],
            dst_ref=pair_dst.at[i],
            send_sem=pair_send.at[i],
            recv_sem=pair_recv.at[i],
            device_id={"hour": me ^ 1},
            device_id_type=pl.DeviceIdType.MESH,
        )

    def pair_up(i, total):
        total_src[i, 0] = total[:hb]
        total_src[i, 1] = total[hb:]
        pair_copy(i).start()

    def broadcast(i):
        pair_copy(i).wait_recv()
        chip = total_src[i, side] + pair_dst[i]
        chip_src[i] = chip
        push(lambda peer: chip_src.at[i], total_dst.at[i], 11 + i)
        total_dst[i, me] = chip

    def capacity_step(i):
        arrive(total_dst.at[i], 11 + i)
        low, high = total_dst[i, 0], total_dst[i, 1]
        for d in range(2, n, 2):
            low = low + total_dst[i, d]
            high = high + total_dst[i, d + 1]
        total = jnp.concatenate([low, high], axis=0)
        old = cap_ref[...]
        trial = next_capacity(old, cost_in[...], total)
        cap_ref[...] = trial
        return 2.0 * trial - old

    for copy in own:
        copy.wait()

    def push_flow(q):
        push(
            lambda peer: flow_hbm.at[peer, pl.ds(q * quarter_lb, quarter_lb)],
            flow_in.at[q],
            (6, 7, 19, 20)[q],
        )

    arrive(upper, 1)
    arrive(grad_dst, 4)
    push_flow(0)
    push_flow(1)
    arrive(lower, 2)
    push_flow(2)
    arrive(power, 3)
    push_flow(3)
    gradient(
        jnp.concatenate([grad_dst[:, j, :] for j in range(bb)], axis=1).astype(jnp.bfloat16)
    )
    adjoints()
    primal(power, adjoint, first_dst, power)
    states()
    arrive(cap_dst, 5)
    cap_ref[...] = cap_dst[:, 0, :]
    pair_up(0, update_duals(cap_dst[:, 1, :]))
    value = inject(0)
    broadcast(0)
    send_injection(0)
    adjoints()
    for c in range(0, lines, width):
        flows1[:, c : c + width] = line_flows(value, c)
    for q in range(4):
        arrive(flow_in.at[q], (6, 7, 19, 20)[q])
        for j in range(quarter_lb):
            flow[:, lanes(q * quarter_lb + j)] = flow_in[q, :, j, :]
        for c in range(q * quarter_lb * 128, (q + 1) * quarter_lb * 128, width):
            advance(flow, c, flows1[:, c : c + width])

    gradient(bus_dual(flow[...]))
    primal(power, adjoint, first_dst, power)
    states()
    pair_up(1, update_duals(capacity_step(0)))
    value = inject(1)
    broadcast(1)
    send_injection(1)
    adjoints()
    lines_step(flow, value)

    gradient(bus_dual(flow[...]))
    primal(power, adjoint, first_dst, power)
    push(lambda peer: power.at[peer], power_home, 14)
    power_home[me] = power[me]
    states()
    part_src[:, 0, :] = update_duals(capacity_step(1))
    push(lambda peer: part_src.at[peer], part_dst, 13)
    part_dst[me] = part_src[me]
    adjoints()
    value = inject(2)
    send_injection(2)
    push(lambda peer: adjoint.at[peer], adjoint_home, 15)
    adjoint_home[me] = adjoint[me]
    lines_step(flow, value)

    gradient(bus_dual(flow[...]))
    primal(power, adjoint, first_dst, None)
    e = start_in[...]
    for t in range(hours):
        e = retain * e - bar[t]
        lower[t] = jnp.maximum(lower[t] - dual_step * e, 0.0)
        upper[t] = upper[t] + dual_step * e
    push(lambda peer: lower.at[peer], lower_out, 16)
    lower_out[me] = lower[me]
    upper_out[me] = upper[me]
    arrive(part_dst, 13)
    old = cap_ref[pl.ds(me, 1), :]
    trial = next_capacity(old, my_cost, jnp.sum(part_dst[:, 0, :], axis=0, keepdims=True))
    capacity_out[...] = trial
    last_src[...] = 2.0 * trial - old
    push(lambda peer: last_src, last_dst, 18)
    push(lambda peer: upper.at[peer], upper_out, 17)
    last_dst[me] = last_src[...]

    lines_step(flow2, injected(0))
    lines_step(flow2, injected(1))
    lines_step(flow2, injected(2))
    gradient(bus_dual(flow2[...]))
    arrive(power_home, 14)
    arrive(adjoint_home, 15)
    primal(power_home, adjoint_home, first_src, power_out)
    lines_step(flow2, injection(grad_src))
    for j in range(lb):
        flow_out[:, j, :] = flow2[:, lanes(j)]
    arrive(lower_out, 16)
    arrive(upper_out, 17)
    arrive(last_dst, 18)
    raised = dual_step * last_dst[:, 0, :]
    for s in range(scen):
        upper_out[s] = jnp.maximum(upper_out[s] - raised, 0.0)
    sent = (
        [first_dst, upper, lower, power, grad_dst, cap_dst, flow_in.at[0], flow_in.at[1]]
        + [inj_dst.at[i] for i in range(3)]
        + [total_dst.at[i] for i in range(2)]
        + [part_dst, power_home, adjoint_home, lower_out, upper_out, last_dst]
        + [flow_in.at[2], flow_in.at[3]]
    )
    for channel, dst in enumerate(sent):
        everything(dst, channel).wait_send()
    for i in range(2):
        pair_copy(i).wait_send()


def by_rows(n, args):
    power, capacity, flow, upper, lower, price, load, shift, limit, bus = args[:10]
    leak, start, plimit, cost = args[10:]
    scen, _, units = power.shape
    lines, buses = shift.shape
    ub, lb, bb = units // 128, lines // 128, buses // 128
    vmem = pl.BlockSpec(memory_space=pltpu.VMEM)
    hbm = pl.BlockSpec(memory_space=pltpu.HBM)
    state, wide = (scen, ub, 128), (scen, lb, 128)
    args = (
        power.reshape(state),
        capacity,
        flow.reshape(wide),
        upper.reshape(state),
        lower.reshape(state),
        price,
        load,
        shift,
        limit,
        bus,
        leak,
        start,
        plimit,
        cost,
    )
    f32 = jnp.float32
    results = tuple(jax.ShapeDtypeStruct(args[i].shape, f32) for i in range(5))

    def buffer(*shape, dtype=f32):
        return pltpu.VMEM(shape, dtype)

    out = pl.pallas_call(
        functools.partial(kernel_rows, n),
        out_shape=results,
        in_specs=[hbm] * 14,
        out_specs=(vmem,) * 5,
        scratch_shapes=[pltpu.VMEM(args[i].shape, args[i].dtype) for i in (1, 2, 3)]
        + [pltpu.VMEM(a.shape, a.dtype) for a in args[5:]]
        + [buffer(buses, units, dtype=jnp.bfloat16)]
        + [buffer(units, buses, dtype=jnp.bfloat16)]
        + [buffer(buses, lines, dtype=jnp.bfloat16)]
        + [buffer(*state)] * 3
        + [buffer(4, n, lb // 4, 128)]
        + [buffer(*state)] * 2
        + [buffer(n, units, dtype=jnp.bfloat16)]
        + [buffer(n, lines)] * 3
        + [
            buffer(n, 2, 128),
            buffer(n, 2, 128),
            buffer(2, 128),
            buffer(n, 2, 128),
            buffer(n, 2 * bb, 128),
            buffer(n, 2 * bb, 128),
            buffer(2, 2, ub // 2, 128),
            buffer(2, ub // 2, 128),
            buffer(2, ub // 2, 128),
            buffer(2, n, ub // 2, 128),
            buffer(n, 1, 128),
            buffer(n, 1, 128),
            buffer(1, 128),
            buffer(n, 1, 128),
            buffer(3, n, bb, 128),
            buffer(3, n, bb, 128),
            buffer(*state),
            buffer(*state),
            buffer(*state),
            buffer(*state),
            buffer(ub, 128),
            pltpu.SemaphoreType.DMA((21,)),
            pltpu.SemaphoreType.DMA((21,)),
            pltpu.SemaphoreType.DMA((2,)),
            pltpu.SemaphoreType.DMA((2,)),
            pltpu.SemaphoreType.DMA((15,)),
            pltpu.SemaphoreType.DMA((7,)),
        ],
        compiler_params=pltpu.CompilerParams(
            collective_id=0, has_side_effects=True, vmem_limit_bytes=48 * 1024 * 1024
        ),
    )(*(pltpu.with_memory_space_constraint(a, pltpu.HBM) for a in args))
    out = pl.pallas_call(
        store,
        out_shape=results,
        in_specs=[vmem] * 5,
        out_specs=(hbm,) * 5,
        scratch_shapes=[pltpu.SemaphoreType.DMA((5,))],
        compiler_params=pltpu.CompilerParams(vmem_limit_bytes=16 * 1024 * 1024),
    )(*out)
    return (
        out[0].reshape(power.shape),
        out[1].reshape(units // n),
        out[2].reshape(flow.shape),
        out[3].reshape(upper.shape),
        out[4].reshape(lower.shape),
    )


def on_device(
    power,
    capacity,
    flow_dual,
    upper_dual,
    lower_dual,
    price,
    load,
    shift_factors,
    line_limit,
    unit_bus,
    leakage,
    initial_state,
    power_limit,
    capacity_cost,
):
    n = lax.axis_size("hour")
    scen, hdev, units = power.shape
    lines, buses = shift_factors.shape
    ud, rows = units // n, scen * hdev
    block = pltpu.VMEM((n, rows, ud), jnp.float32)
    vmem = pl.BlockSpec(memory_space=pltpu.VMEM)
    hbm = pl.BlockSpec(memory_space=pltpu.HBM)
    args = (
        power,
        capacity.reshape(1, ud),
        flow_dual,
        upper_dual,
        lower_dual,
        price.T,
        load.transpose(1, 0, 2),
        shift_factors,
        line_limit.reshape(1, lines),
        unit_bus.reshape(1, units),
        leakage.reshape(n, ud),
        initial_state.reshape(n, ud),
        power_limit.reshape(n, ud),
        capacity_cost.reshape(n, ud),
    )
    if scen == n and hdev == 1 and ud == 128 and lines % 1024 == 0 and buses % 128 == 0:
        return by_rows(n, args)
    results = tuple(
        jax.ShapeDtypeStruct(args[i].shape, jnp.float32) for i in range(5)
    )
    out = pl.pallas_call(
        functools.partial(kernel, n),
        out_shape=results,
        in_specs=[hbm] * 14,
        out_specs=(vmem,) * 5,
        scratch_shapes=[pltpu.VMEM(a.shape, a.dtype) for a in args]
        + [
            pltpu.VMEM((buses, units), jnp.bfloat16),
            block,
            block,
            pltpu.VMEM((rows, lines), jnp.float32),
            pltpu.VMEM((rows, units), jnp.bfloat16),
        ]
        + [block] * 8
        + [
            pltpu.SemaphoreType.DMA((4, n)),
            pltpu.SemaphoreType.DMA((4, n)),
            pltpu.SemaphoreType.DMA((14,)),
        ],
        compiler_params=pltpu.CompilerParams(
            collective_id=0, has_side_effects=True, vmem_limit_bytes=48 * 1024 * 1024
        ),
    )(*(pltpu.with_memory_space_constraint(a, pltpu.HBM) for a in args))
    out = pl.pallas_call(
        store,
        out_shape=results,
        in_specs=[vmem] * 5,
        out_specs=(hbm,) * 5,
        scratch_shapes=[pltpu.SemaphoreType.DMA((5,))],
        compiler_params=pltpu.CompilerParams(vmem_limit_bytes=16 * 1024 * 1024),
    )(*out)
    return (out[0], out[1].reshape(ud), out[2], out[3], out[4])


def solution(mesh):
    return jax.shard_map(
        on_device,
        mesh=mesh,
        in_specs=(
            P("groups", "hour", None),
            P(("groups", "hour")),
            P("groups", "hour", None),
            P("groups", "hour", None),
            P("groups", "hour", None),
            P("groups", "hour"),
            P("groups", "hour", None),
            P(),
            P(),
            P(),
            P(),
            P("groups"),
            P(),
            P(),
        ),
        out_specs=(
            P("groups", "hour", None),
            P(("groups", "hour")),
            P("groups", "hour", None),
            P("groups", "hour", None),
            P("groups", "hour", None),
        ),
        check_vma=False,
    )
```

```python
import functools

import jax
import jax.numpy as jnp
from jax import lax
from jax.experimental import pallas as pl
from jax.experimental.pallas import tpu as pltpu
from jax.sharding import PartitionSpec as P

ITERS = 4

primal_step = 0.05
dual_step = 0.01


def kernel(n, *refs):
    arrived, refs = refs[:14], refs[14:]
    (power_out, capacity_out, flow_out, upper_out, lower_out), refs = refs[:5], refs[5:]
    held, refs = refs[:14], refs[14:]
    (
        power_in,
        capacity_in,
        flow_in,
        upper_in,
        lower_in,
        price_in,
        load_in,
        shift,
        limit_in,
        bus_in,
        leak_in,
        start_in,
        plimit_in,
        cost_in,
    ) = held
    (
        inc,
        power,
        grid,
        flow,
        bar16,
        upper,
        lower,
        upper_stage,
        lower_stage,
        adj,
        adj_got,
        bar,
        bar_got,
        send_sems,
        recv_sems,
        load_sems,
    ) = refs
    me = lax.axis_index("hour")
    scen, hdev, units = power_in.shape
    lines, buses = shift.shape
    ud = units // n
    hours = hdev * n
    loads = [
        pltpu.make_async_copy(src, dst, load_sems.at[i])
        for i, (src, dst) in enumerate(zip(arrived, held))
    ]
    first = (3, 4)
    for i in first:
        loads[i].start()

    def peer_of(k):
        return me ^ k

    def copy_to(src, dst, channel, peer):
        return pltpu.make_async_remote_copy(
            src_ref=src.at[peer],
            dst_ref=dst.at[me],
            send_sem=send_sems.at[channel, peer],
            recv_sem=recv_sems.at[channel, me],
            device_id={"hour": peer},
            device_id_type=pl.DeviceIdType.MESH,
        )

    def wait_from(dst, channel, source):
        pltpu.make_async_remote_copy(
            src_ref=dst.at[source],
            dst_ref=dst.at[source],
            send_sem=send_sems.at[channel, source],
            recv_sem=recv_sems.at[channel, source],
            device_id={"hour": source},
            device_id_type=pl.DeviceIdType.MESH,
        ).wait_recv()

    blocks = sorted(range(1, n // 4), key=lambda z: -min(z, n // 4 - z))
    order = [z * 4 + low for low in (2, 3, 0, 1) for z in blocks] + [2, 3, 1]
    assert n % 4 == 0 and n & (n - 1) == 0 and sorted(order) == list(range(1, n))

    def each(order, function):
        for k in order:
            function(k)

    def rows_of(ref, lanes):
        return jnp.concatenate([ref[:, j, lanes] for j in range(hdev)], axis=0)

    barrier = pltpu.get_barrier_semaphore()
    each(
        order,
        lambda k: pl.semaphore_signal(
            barrier,
            inc=1,
            device_id={"hour": peer_of(k)},
            device_id_type=pl.DeviceIdType.MESH,
        ),
    )
    for i in (9, 0, 2, 7, 1, 5, 6, 8, 10, 11, 12, 13):
        loads[i].start()
    for i in first:
        loads[i].wait()
    for d in range(n):
        lanes = slice(d * ud, (d + 1) * ud)
        upper_stage[d] = rows_of(upper_in, lanes)
        lower_stage[d] = upper_stage[d] - rows_of(lower_in, lanes)
    pl.semaphore_wait(barrier, n - 1)

    each(order, lambda k: copy_to(lower_stage, lower, 1, peer_of(k)).start())
    each(order, lambda k: copy_to(upper_stage, upper, 0, peer_of(k)).start())
    upper[me] = upper_stage[me]
    lower[me] = lower_stage[me]
    for i in range(14):
        if i not in first and i != 7:
            loads[i].wait()
    for d in range(n):
        power[d] = rows_of(power_in, slice(d * ud, (d + 1) * ud))
    for j in range(hdev):
        flow[j * scen : (j + 1) * scen, :] = flow_in[:, j, :]
    piece = 128
    names = bus_in[...]
    for b in range(0, buses, piece):
        rows = lax.broadcasted_iota(jnp.int32, (piece, units), 0) + b
        inc[b : b + piece, :] = jnp.where(rows == names, 1.0, 0.0).astype(jnp.bfloat16)
    capacity_out[...] = capacity_in[...]
    retain = 1.0 - leak_in[pl.ds(me, 1), :]
    begin = start_in[pl.ds(me, 1), :]
    cost = cost_in[pl.ds(me, 1), :]
    eye = lax.broadcasted_iota(jnp.int32, (scen, scen), 0) == lax.broadcasted_iota(
        jnp.int32, (scen, scen), 1
    )
    price = jnp.concatenate(
        [
            jnp.sum(jnp.where(eye, price_in[j : j + 1, :], 0.0), axis=1, keepdims=True)
            for j in range(hdev)
        ],
        axis=0,
    )
    loads[7].wait()

    def place(t):
        return t // hdev, slice((t % hdev) * scen, (t % hdev + 1) * scen)

    def adjoint(difference):
        w = jnp.zeros((scen, ud), jnp.float32)
        for t in reversed(range(hours)):
            d, rows = place(t)
            w = retain * w + difference(d, rows)
            adj[d, rows, :] = w
        each(order, lambda k: copy_to(adj, adj_got, 2, peer_of(k)).start())
        adj_got[me] = adj[me]

    def iteration(first):
        bus_dual = jnp.dot(
            flow[...].astype(jnp.bfloat16), shift[...], preferred_element_type=jnp.float32
        ).astype(jnp.bfloat16)
        grid_grad = jnp.dot(bus_dual, inc[...], preferred_element_type=jnp.float32)
        for d in range(n):
            grid[d] = grid_grad[:, d * ud : (d + 1) * ud]

        def advance(d):
            limit = plimit_in[pl.ds(d, 1), :]
            old = power[d]
            trial = jnp.clip(
                old - primal_step * (grid[d] - adj_got[d] - price), -limit, limit
            )
            bar[d] = 2.0 * trial - old
            power[d] = trial

        advance(me)
        bar_got[me] = bar[me]

        def answer(k):
            source = peer_of(k)
            wait_from(adj_got, 2, source)
            advance(source)
            copy_to(bar, bar_got, 3, source).start()

        each(order, answer)
        for d in range(n):
            bar16[:, d * ud : (d + 1) * ud] = bar[d].astype(jnp.bfloat16)
        injection = lax.dot_general(
            bar16[...], inc[...], (((1,), (1,)), ((), ())), preferred_element_type=jnp.float32
        )
        load = jnp.concatenate([load_in[j] for j in range(hdev)], axis=0)
        injection = (injection - load.astype(jnp.float32)).astype(jnp.bfloat16)
        width = min(1024, lines)
        for c in range(0, lines, width):
            flows = lax.dot_general(
                injection,
                shift[c : c + width, :],
                (((1,), (1,)), ((), ())),
                preferred_element_type=jnp.float32,
            )
            probe = flow[:, c : c + width] + dual_step * flows
            edge = dual_step * limit_in[:, c : c + width]
            flow[:, c : c + width] = probe - jnp.clip(probe, -edge, edge)

        if first:

            def wait_upper(k):
                wait_from(upper, 0, peer_of(k))
                copy_to(upper_stage, upper, 0, peer_of(k)).wait_send()
                copy_to(lower_stage, lower, 1, peer_of(k)).wait_send()

            each(order, wait_upper)
            for d in range(n):
                lower[d] = upper[d] - lower[d]
        total = jnp.zeros((scen, ud), jnp.float32)
        for t in range(hours):
            d, rows = place(t)
            total = total + upper[d, rows, :]
        dual_total = jnp.sum(total, axis=0, keepdims=True)
        capacity = capacity_out[...]
        trial_capacity = jnp.maximum(
            capacity - primal_step * (hours * cost - dual_total / scen), 0.0
        )
        capacity_bar = 2.0 * trial_capacity - capacity
        capacity_out[...] = trial_capacity

        def wait_bar(k):
            wait_from(bar_got, 3, peer_of(k))
            copy_to(adj, adj_got, 2, peer_of(k)).wait_send()
            copy_to(bar, bar_got, 3, peer_of(k)).wait_send()

        each(order, wait_bar)
        e = jnp.broadcast_to(begin, (scen, ud))
        for t in range(hours):
            d, rows = place(t)
            e = retain * e - bar_got[d, rows, :]
            upper[d, rows, :] = jnp.maximum(
                upper[d, rows, :] + dual_step * (e - capacity_bar), 0.0
            )
            lower[d, rows, :] = jnp.maximum(lower[d, rows, :] - dual_step * e, 0.0)

    each(order, lambda k: wait_from(lower, 1, peer_of(k)))
    adjoint(lambda d, rows: lower[d, rows, :])
    iteration(True)

    def again(step, carry):
        adjoint(lambda d, rows: upper[d, rows, :] - lower[d, rows, :])
        iteration(False)
        return carry

    lax.fori_loop(1, ITERS, again, 0)

    def send_last(k):
        copy_to(upper, adj_got, 2, peer_of(k)).start()
        copy_to(lower, lower_stage, 0, peer_of(k)).start()

    each(order, send_last)
    adj_got[me] = upper[me]
    lower_stage[me] = lower[me]
    for d in range(n):
        for j in range(hdev):
            power_out[:, j, d * ud : (d + 1) * ud] = power[d, j * scen : (j + 1) * scen, :]
    for j in range(hdev):
        flow_out[:, j, :] = flow[j * scen : (j + 1) * scen, :]

    def wait_last(k):
        wait_from(adj_got, 2, peer_of(k))
        wait_from(lower_stage, 0, peer_of(k))
        copy_to(upper, adj_got, 2, peer_of(k)).wait_send()
        copy_to(lower, lower_stage, 0, peer_of(k)).wait_send()

    each(order, wait_last)
    for d in range(n):
        for j in range(hdev):
            lanes, rows = slice(d * ud, (d + 1) * ud), slice(j * scen, (j + 1) * scen)
            upper_out[:, j, lanes] = adj_got[d, rows, :]
            lower_out[:, j, lanes] = lower_stage[d, rows, :]


def store(*refs):
    sems = refs[10]
    copies = [
        pltpu.make_async_copy(refs[i], refs[5 + i], sems.at[i]) for i in (2, 0, 3, 4, 1)
    ]
    for copy in copies:
        copy.start()
    for copy in copies:
        copy.wait()


def kernel_rows(n, *refs):
    hbm, refs = refs[:14], refs[14:]
    (power_out, capacity_out, flow_out, upper_out, lower_out), refs = refs[:5], refs[5:]
    (
        capacity_in,
        flow_home,
        upper_home,
        price_in,
        load_in,
        shift,
        limit_in,
        bus_in,
        leak_in,
        start_in,
        plimit_in,
        cost_in,
        inc,
        inc_t,
        shift_t,
        upper,
        lower,
        power,
        flow_in,
        grid,
        bar,
        bar16,
        flow,
        flow2,
        flows1,
        first_src,
        first_dst,
        cap_src,
        cap_dst,
        grad_src,
        grad_dst,
        total_src,
        pair_dst,
        chip_src,
        total_dst,
        part_src,
        part_dst,
        last_src,
        last_dst,
        inj_src,
        inj_dst,
        state,
        power_home,
        adjoint,
        adjoint_home,
        cap_ref,
        send_sems,
        recv_sems,
        pair_send,
        pair_recv,
        load_sems,
        own_sems,
    ) = refs
    me = lax.axis_index("hour")
    power_hbm, flow_hbm, upper_hbm, lower_hbm = hbm[0], hbm[2], hbm[3], hbm[4]
    hours = scen = n
    lines, buses = shift.shape
    ub, lb, bb = upper_home.shape[1], flow_home.shape[1], buses // 128
    quarter_lb = lb // 4
    units = ub * 128

    blocks = sorted(range(1, n // 4), key=lambda z: -min(z, n // 4 - z))
    order = [z * 4 + low for low in (2, 3, 0, 1) for z in blocks] + [2, 3, 1]
    assert n % 4 == 0 and n & (n - 1) == 0 and sorted(order) == list(range(1, n))

    barrier = pltpu.get_barrier_semaphore()
    for k in reversed(range(1, n)):
        pl.semaphore_signal(
            barrier,
            inc=1,
            device_id={"hour": me ^ k},
            device_id_type=pl.DeviceIdType.MESH,
        )
    loads = {}

    def load(name, src, dst, i):
        loads[name] = pltpu.make_async_copy(src, dst, load_sems.at[i])
        loads[name].start()

    load("upper", upper_hbm, upper_home, 0)
    load("price", hbm[5], price_in, 1)
    load("flow", flow_hbm, flow_home, 2)
    quarter = lines // 4
    for q in range(4):
        rows = pl.ds(q * quarter, quarter)
        load(("shift", q), hbm[7].at[rows], shift.at[rows], 3 + q)

    for i, (name, src, dst) in enumerate(
        (
            ("load", 6, load_in),
            ("bus", 9, bus_in),
            ("capacity", 1, capacity_in),
            ("cost", 13, cost_in),
            ("leak", 10, leak_in),
            ("plimit", 12, plimit_in),
            ("start", 11, start_in),
            ("limit", 8, limit_in),
        )
    ):
        load(name, hbm[src], dst, 7 + i)
    own = [
        pltpu.make_async_copy(src, dst.at[me], own_sems.at[i])
        for i, (src, dst) in enumerate(
            (
                (upper_hbm.at[me], upper),
                (lower_hbm.at[me], lower),
                (power_hbm.at[me], power),
            )
            + tuple(
                (flow_hbm.at[me, pl.ds(q * quarter_lb, quarter_lb)], flow_in.at[q])
                for q in range(4)
            )
        )
    ]
    for copy in own:
        copy.start()

    def push(source, dst, channel):
        for k in order:
            peer = me ^ k
            pltpu.make_async_remote_copy(
                src_ref=source(peer),
                dst_ref=dst.at[me],
                send_sem=send_sems.at[channel],
                recv_sem=recv_sems.at[channel],
                device_id={"hour": peer},
                device_id_type=pl.DeviceIdType.MESH,
            ).start()

    def everything(dst, channel):
        rest = dst.at[pl.ds(0, n - 1)]
        return pltpu.make_async_remote_copy(
            src_ref=rest,
            dst_ref=rest,
            send_sem=send_sems.at[channel],
            recv_sem=recv_sems.at[channel],
            device_id={"hour": me ^ 1},
            device_id_type=pl.DeviceIdType.MESH,
        )

    def arrive(dst, channel):
        everything(dst, channel).wait_recv()

    def lanes(j):
        return slice(j * 128, (j + 1) * 128)

    eye = lax.broadcasted_iota(jnp.int32, (scen, scen), 0) == lax.broadcasted_iota(
        jnp.int32, (scen, scen), 1
    )
    loads["upper"].wait()
    loads["price"].wait()
    part = upper_home[0]
    for s in range(1, scen):
        part = part + upper_home[s]
    price = jnp.sum(jnp.where(eye, price_in[...], 0.0), axis=1, keepdims=True)
    first_src[:, 0, :] = part
    first_src[:, 1, :] = jnp.broadcast_to(price, (scen, 128))
    pl.semaphore_wait(barrier, n - 1)

    push(lambda peer: first_src.at[peer], first_dst, 0)
    push(lambda peer: upper_hbm.at[peer], upper, 1)
    first_dst[me] = first_src[me]

    def bus_dual(rows):
        return jnp.dot(
            rows.astype(jnp.bfloat16), shift[...], preferred_element_type=jnp.float32
        ).astype(jnp.bfloat16)

    loads["flow"].wait()
    for j in range(lb):
        flow2[:, lanes(j)] = flow_home[:, j, :]
    for q in range(4):
        loads[("shift", q)].wait()
    dual = bus_dual(flow2[...]).astype(jnp.float32)
    loads["load"].wait()
    demand = load_in[0].astype(jnp.float32)
    for j in range(bb):
        grad_src[:, j, :] = dual[:, lanes(j)]
        grad_src[:, bb + j, :] = demand[:, lanes(j)]
    push(lambda peer: grad_src.at[peer], grad_dst, 4)
    push(lambda peer: lower_hbm.at[peer], lower, 2)
    grad_dst[me] = grad_src[me]

    loads["capacity"].wait()
    loads["cost"].wait()
    arrive(first_dst, 0)
    my_cost = cost_in[pl.ds(me, 1), :]

    def next_capacity(old, cost, total):
        return jnp.maximum(old - primal_step * (hours * cost - total / scen), 0.0)

    old = capacity_in[...]
    trial = next_capacity(old, my_cost, jnp.sum(first_dst[:, 0, :], axis=0, keepdims=True))
    cap_src[0:1, :] = trial
    cap_src[1:2, :] = 2.0 * trial - old
    push(lambda peer: cap_src, cap_dst, 5)
    cap_dst[me] = cap_src[...]
    push(lambda peer: power_hbm.at[peer], power, 3)

    for name in ("bus", "leak", "plimit", "start", "limit"):
        loads[name].wait()
    piece = 128
    names = bus_in[...]
    for b in range(0, buses, piece):
        rows = lax.broadcasted_iota(jnp.int32, (piece, units), 0) + b
        inc[b : b + piece, :] = jnp.where(rows == names, 1.0, 0.0).astype(jnp.bfloat16)
    retain = 1.0 - leak_in[...]
    plimit = plimit_in[...]
    for b in range(0, buses, piece):
        inc_t[:, b : b + piece] = inc[b : b + piece, :].T
    for c in range(0, lines, 512):
        shift_t[:, c : c + 512] = shift[c : c + 512, :].T
    width = min(1024, lines)

    def gradient(dual):
        value = jnp.dot(dual, inc[...], preferred_element_type=jnp.float32)
        for j in range(ub):
            grid[:, j, :] = value[:, lanes(j)]

    def adjoints():
        w = jnp.zeros((ub, 128), jnp.float32)
        for t in reversed(range(hours)):
            w = retain * w + (upper[t] - lower[t])
            adjoint[t] = w

    def primal(old_from, dual_from, prices, new_to):
        for t in range(hours):
            old = old_from[t]
            trial = jnp.clip(
                old - primal_step * (grid[t] - dual_from[t] - prices[t, 1:2, :]),
                -plimit,
                plimit,
            )
            bar[t] = 2.0 * trial - old
            if new_to is not None:
                new_to[t] = trial

    def states():
        e = start_in[...]
        for t in range(hours):
            e = retain * e - bar[t]
            state[t] = e

    def injection(demand_from):
        for j in range(ub):
            bar16[:, lanes(j)] = bar[:, j, :].astype(jnp.bfloat16)
        value = jnp.dot(bar16[...], inc_t[...], preferred_element_type=jnp.float32)
        demand = jnp.concatenate([demand_from[:, bb + j, :] for j in range(bb)], axis=1)
        return (value - demand).astype(jnp.bfloat16)

    def inject(i):
        value = injection(grad_dst)
        wide = value.astype(jnp.float32)
        for j in range(bb):
            inj_src[i, :, j, :] = wide[:, lanes(j)]
        return value

    def send_injection(i):
        push(lambda peer: inj_src.at[i, peer], inj_dst.at[i], 8 + i)
        inj_dst[i, me] = inj_src[i, me]

    def injected(i):
        arrive(inj_dst.at[i], 8 + i)
        return jnp.concatenate([inj_dst[i, :, j, :] for j in range(bb)], axis=1).astype(
            jnp.bfloat16
        )

    def line_flows(value, c):
        return jnp.dot(value, shift_t[:, c : c + width], preferred_element_type=jnp.float32)

    def advance(ref, c, flows):
        probe = ref[:, c : c + width] + dual_step * flows
        edge = dual_step * limit_in[:, c : c + width]
        ref[:, c : c + width] = probe - jnp.clip(probe, -edge, edge)

    def lines_step(ref, value):
        for c in range(0, lines, width):
            advance(ref, c, line_flows(value, c))

    def partial_dual(ref, c):
        return jnp.dot(
            ref[:, c : c + width].astype(jnp.bfloat16),
            shift[c : c + width, :],
            preferred_element_type=jnp.float32,
        )

    def flow_step(ref, value):
        dual = jnp.zeros((n, buses), jnp.float32)
        for c in range(0, lines, width):
            advance(ref, c, line_flows(value, c))
            dual = dual + partial_dual(ref, c)
        return dual.astype(jnp.bfloat16)

    def update_duals(capacity_bar):
        total = jnp.zeros((ub, 128), jnp.float32)
        for t in range(hours):
            e = state[t]
            raised = jnp.maximum(upper[t] + dual_step * (e - capacity_bar), 0.0)
            upper[t] = raised
            total = total + raised
            lower[t] = jnp.maximum(lower[t] - dual_step * e, 0.0)
        return total

    hb = ub // 2
    side = me % 2

    def pair_copy(i):
        return pltpu.make_async_remote_copy(
            src_ref=total_src.at[i, 1 - side],
            dst_ref=pair_dst.at[i],
            send_sem=pair_send.at[i],
            recv_sem=pair_recv.at[i],
            device_id={"hour": me ^ 1},
            device_id_type=pl.DeviceIdType.MESH,
        )

    def pair_up(i, total):
        total_src[i, 0] = total[:hb]
        total_src[i, 1] = total[hb:]
        pair_copy(i).start()

    def broadcast(i):
        pair_copy(i).wait_recv()
        chip = total_src[i, side] + pair_dst[i]
        chip_src[i] = chip
        push(lambda peer: chip_src.at[i], total_dst.at[i], 11 + i)
        total_dst[i, me] = chip

    def capacity_step(i):
        arrive(total_dst.at[i], 11 + i)
        low, high = total_dst[i, 0], total_dst[i, 1]
        for d in range(2, n, 2):
            low = low + total_dst[i, d]
            high = high + total_dst[i, d + 1]
        total = jnp.concatenate([low, high], axis=0)
        old = cap_ref[...]
        trial = next_capacity(old, cost_in[...], total)
        cap_ref[...] = trial
        return 2.0 * trial - old

    for copy in own:
        copy.wait()

    def push_flow(q):
        push(
            lambda peer: flow_hbm.at[peer, pl.ds(q * quarter_lb, quarter_lb)],
            flow_in.at[q],
            (6, 7, 19, 20)[q],
        )

    arrive(upper, 1)
    arrive(grad_dst, 4)
    push_flow(0)
    arrive(lower, 2)
    push_flow(1)
    push_flow(2)
    push_flow(3)
    arrive(power, 3)
    gradient(
        jnp.concatenate([grad_dst[:, j, :] for j in range(bb)], axis=1).astype(jnp.bfloat16)
    )
    adjoints()
    primal(power, adjoint, first_dst, power)
    states()
    arrive(cap_dst, 5)
    cap_ref[...] = cap_dst[:, 0, :]
    pair_up(0, update_duals(cap_dst[:, 1, :]))
    value = inject(0)
    broadcast(0)
    adjoints()
    for c in range(0, lines, width):
        flows1[:, c : c + width] = line_flows(value, c)
    dual = jnp.zeros((n, buses), jnp.float32)
    for q in range(4):
        arrive(flow_in.at[q], (6, 7, 19, 20)[q])
        for j in range(quarter_lb):
            flow[:, lanes(q * quarter_lb + j)] = flow_in[q, :, j, :]
        for c in range(q * quarter_lb * 128, (q + 1) * quarter_lb * 128, width):
            advance(flow, c, flows1[:, c : c + width])
            dual = dual + partial_dual(flow, c)

    gradient(dual.astype(jnp.bfloat16))
    primal(power, adjoint, first_dst, power)
    send_injection(0)
    states()
    pair_up(1, update_duals(capacity_step(0)))
    value = inject(1)
    broadcast(1)
    send_injection(1)
    adjoints()
    gradient(flow_step(flow, value))
    primal(power, adjoint, first_dst, power)
    push(lambda peer: power.at[peer], power_home, 14)
    power_home[me] = power[me]
    states()
    lines_step(flow2, injected(0))
    part_src[:, 0, :] = update_duals(capacity_step(1))
    push(lambda peer: part_src.at[peer], part_dst, 13)
    part_dst[me] = part_src[me]
    adjoints()
    value = inject(2)
    send_injection(2)
    push(lambda peer: adjoint.at[peer], adjoint_home, 15)
    adjoint_home[me] = adjoint[me]
    gradient(flow_step(flow, value))
    primal(power, adjoint, first_dst, None)
    e = start_in[...]
    for t in range(hours):
        e = retain * e - bar[t]
        lower[t] = jnp.maximum(lower[t] - dual_step * e, 0.0)
        upper[t] = upper[t] + dual_step * e
    push(lambda peer: lower.at[peer], lower_out, 16)
    lower_out[me] = lower[me]
    upper_out[me] = upper[me]
    lines_step(flow2, injected(1))
    arrive(part_dst, 13)
    old = cap_ref[pl.ds(me, 1), :]
    trial = next_capacity(old, my_cost, jnp.sum(part_dst[:, 0, :], axis=0, keepdims=True))
    capacity_out[...] = trial
    last_src[...] = 2.0 * trial - old
    push(lambda peer: last_src, last_dst, 18)
    push(lambda peer: upper.at[peer], upper_out, 17)
    last_dst[me] = last_src[...]

    gradient(flow_step(flow2, injected(2)))
    arrive(power_home, 14)
    arrive(adjoint_home, 15)
    primal(power_home, adjoint_home, first_src, power_out)
    lines_step(flow2, injection(grad_src))
    for j in range(lb):
        flow_out[:, j, :] = flow2[:, lanes(j)]
    arrive(lower_out, 16)
    arrive(upper_out, 17)
    arrive(last_dst, 18)
    raised = dual_step * last_dst[:, 0, :]
    for s in range(scen):
        upper_out[s] = jnp.maximum(upper_out[s] - raised, 0.0)
    sent = (
        [first_dst, upper, lower, power, grad_dst, cap_dst, flow_in.at[0], flow_in.at[1]]
        + [inj_dst.at[i] for i in range(3)]
        + [total_dst.at[i] for i in range(2)]
        + [part_dst, power_home, adjoint_home, lower_out, upper_out, last_dst]
        + [flow_in.at[2], flow_in.at[3]]
    )
    for channel, dst in enumerate(sent):
        everything(dst, channel).wait_send()
    for i in range(2):
        pair_copy(i).wait_send()


def by_rows(n, args):
    power, capacity, flow, upper, lower, price, load, shift, limit, bus = args[:10]
    leak, start, plimit, cost = args[10:]
    scen, _, units = power.shape
    lines, buses = shift.shape
    ub, lb, bb = units // 128, lines // 128, buses // 128
    vmem = pl.BlockSpec(memory_space=pltpu.VMEM)
    hbm = pl.BlockSpec(memory_space=pltpu.HBM)
    state, wide = (scen, ub, 128), (scen, lb, 128)
    args = (
        power.reshape(state),
        capacity,
        flow.reshape(wide),
        upper.reshape(state),
        lower.reshape(state),
        price,
        load,
        shift,
        limit,
        bus,
        leak,
        start,
        plimit,
        cost,
    )
    f32 = jnp.float32
    results = tuple(jax.ShapeDtypeStruct(args[i].shape, f32) for i in range(5))

    def buffer(*shape, dtype=f32):
        return pltpu.VMEM(shape, dtype)

    out = pl.pallas_call(
        functools.partial(kernel_rows, n),
        out_shape=results,
        in_specs=[hbm] * 14,
        out_specs=(vmem,) * 5,
        scratch_shapes=[pltpu.VMEM(args[i].shape, args[i].dtype) for i in (1, 2, 3)]
        + [pltpu.VMEM(a.shape, a.dtype) for a in args[5:]]
        + [buffer(buses, units, dtype=jnp.bfloat16)]
        + [buffer(units, buses, dtype=jnp.bfloat16)]
        + [buffer(buses, lines, dtype=jnp.bfloat16)]
        + [buffer(*state)] * 3
        + [buffer(4, n, lb // 4, 128)]
        + [buffer(*state)] * 2
        + [buffer(n, units, dtype=jnp.bfloat16)]
        + [buffer(n, lines)] * 3
        + [
            buffer(n, 2, 128),
            buffer(n, 2, 128),
            buffer(2, 128),
            buffer(n, 2, 128),
            buffer(n, 2 * bb, 128),
            buffer(n, 2 * bb, 128),
            buffer(2, 2, ub // 2, 128),
            buffer(2, ub // 2, 128),
            buffer(2, ub // 2, 128),
            buffer(2, n, ub // 2, 128),
            buffer(n, 1, 128),
            buffer(n, 1, 128),
            buffer(1, 128),
            buffer(n, 1, 128),
            buffer(3, n, bb, 128),
            buffer(3, n, bb, 128),
            buffer(*state),
            buffer(*state),
            buffer(*state),
            buffer(*state),
            buffer(ub, 128),
            pltpu.SemaphoreType.DMA((21,)),
            pltpu.SemaphoreType.DMA((21,)),
            pltpu.SemaphoreType.DMA((2,)),
            pltpu.SemaphoreType.DMA((2,)),
            pltpu.SemaphoreType.DMA((15,)),
            pltpu.SemaphoreType.DMA((7,)),
        ],
        compiler_params=pltpu.CompilerParams(
            collective_id=0, has_side_effects=True, vmem_limit_bytes=48 * 1024 * 1024
        ),
    )(*(pltpu.with_memory_space_constraint(a, pltpu.HBM) for a in args))
    out = pl.pallas_call(
        store,
        out_shape=results,
        in_specs=[vmem] * 5,
        out_specs=(hbm,) * 5,
        scratch_shapes=[pltpu.SemaphoreType.DMA((5,))],
        compiler_params=pltpu.CompilerParams(vmem_limit_bytes=16 * 1024 * 1024),
    )(*out)
    return (
        out[0].reshape(power.shape),
        out[1].reshape(units // n),
        out[2].reshape(flow.shape),
        out[3].reshape(upper.shape),
        out[4].reshape(lower.shape),
    )


def on_device(
    power,
    capacity,
    flow_dual,
    upper_dual,
    lower_dual,
    price,
    load,
    shift_factors,
    line_limit,
    unit_bus,
    leakage,
    initial_state,
    power_limit,
    capacity_cost,
):
    n = lax.axis_size("hour")
    scen, hdev, units = power.shape
    lines, buses = shift_factors.shape
    ud, rows = units // n, scen * hdev
    block = pltpu.VMEM((n, rows, ud), jnp.float32)
    vmem = pl.BlockSpec(memory_space=pltpu.VMEM)
    hbm = pl.BlockSpec(memory_space=pltpu.HBM)
    args = (
        power,
        capacity.reshape(1, ud),
        flow_dual,
        upper_dual,
        lower_dual,
        price.T,
        load.transpose(1, 0, 2),
        shift_factors,
        line_limit.reshape(1, lines),
        unit_bus.reshape(1, units),
        leakage.reshape(n, ud),
        initial_state.reshape(n, ud),
        power_limit.reshape(n, ud),
        capacity_cost.reshape(n, ud),
    )
    if scen == n and hdev == 1 and ud == 128 and lines % 1024 == 0 and buses % 128 == 0:
        return by_rows(n, args)
    results = tuple(
        jax.ShapeDtypeStruct(args[i].shape, jnp.float32) for i in range(5)
    )
    out = pl.pallas_call(
        functools.partial(kernel, n),
        out_shape=results,
        in_specs=[hbm] * 14,
        out_specs=(vmem,) * 5,
        scratch_shapes=[pltpu.VMEM(a.shape, a.dtype) for a in args]
        + [
            pltpu.VMEM((buses, units), jnp.bfloat16),
            block,
            block,
            pltpu.VMEM((rows, lines), jnp.float32),
            pltpu.VMEM((rows, units), jnp.bfloat16),
        ]
        + [block] * 8
        + [
            pltpu.SemaphoreType.DMA((4, n)),
            pltpu.SemaphoreType.DMA((4, n)),
            pltpu.SemaphoreType.DMA((14,)),
        ],
        compiler_params=pltpu.CompilerParams(
            collective_id=0, has_side_effects=True, vmem_limit_bytes=48 * 1024 * 1024
        ),
    )(*(pltpu.with_memory_space_constraint(a, pltpu.HBM) for a in args))
    out = pl.pallas_call(
        store,
        out_shape=results,
        in_specs=[vmem] * 5,
        out_specs=(hbm,) * 5,
        scratch_shapes=[pltpu.SemaphoreType.DMA((5,))],
        compiler_params=pltpu.CompilerParams(vmem_limit_bytes=16 * 1024 * 1024),
    )(*out)
    return (out[0], out[1].reshape(ud), out[2], out[3], out[4])


def solution(mesh):
    return jax.shard_map(
        on_device,
        mesh=mesh,
        in_specs=(
            P("groups", "hour", None),
            P(("groups", "hour")),
            P("groups", "hour", None),
            P("groups", "hour", None),
            P("groups", "hour", None),
            P("groups", "hour"),
            P("groups", "hour", None),
            P(),
            P(),
            P(),
            P(),
            P("groups"),
            P(),
            P(),
        ),
        out_specs=(
            P("groups", "hour", None),
            P(("groups", "hour")),
            P("groups", "hour", None),
            P("groups", "hour", None),
            P("groups", "hour", None),
        ),
        check_vma=False,
    )
```

```python
import functools

import jax
import jax.numpy as jnp
from jax import lax
from jax.experimental import pallas as pl
from jax.experimental.pallas import tpu as pltpu
from jax.sharding import PartitionSpec as P

ITERS = 4

primal_step = 0.05
dual_step = 0.01


def kernel(n, *refs):
    arrived, refs = refs[:14], refs[14:]
    (power_out, capacity_out, flow_out, upper_out, lower_out), refs = refs[:5], refs[5:]
    held, refs = refs[:14], refs[14:]
    (
        power_in,
        capacity_in,
        flow_in,
        upper_in,
        lower_in,
        price_in,
        load_in,
        shift,
        limit_in,
        bus_in,
        leak_in,
        start_in,
        plimit_in,
        cost_in,
    ) = held
    (
        inc,
        power,
        grid,
        flow,
        bar16,
        upper,
        lower,
        upper_stage,
        lower_stage,
        adj,
        adj_got,
        bar,
        bar_got,
        send_sems,
        recv_sems,
        load_sems,
    ) = refs
    me = lax.axis_index("hour")
    scen, hdev, units = power_in.shape
    lines, buses = shift.shape
    ud = units // n
    hours = hdev * n
    loads = [
        pltpu.make_async_copy(src, dst, load_sems.at[i])
        for i, (src, dst) in enumerate(zip(arrived, held))
    ]
    first = (3, 4)
    for i in first:
        loads[i].start()

    def peer_of(k):
        return me ^ k

    def copy_to(src, dst, channel, peer):
        return pltpu.make_async_remote_copy(
            src_ref=src.at[peer],
            dst_ref=dst.at[me],
            send_sem=send_sems.at[channel, peer],
            recv_sem=recv_sems.at[channel, me],
            device_id={"hour": peer},
            device_id_type=pl.DeviceIdType.MESH,
        )

    def wait_from(dst, channel, source):
        pltpu.make_async_remote_copy(
            src_ref=dst.at[source],
            dst_ref=dst.at[source],
            send_sem=send_sems.at[channel, source],
            recv_sem=recv_sems.at[channel, source],
            device_id={"hour": source},
            device_id_type=pl.DeviceIdType.MESH,
        ).wait_recv()

    blocks = sorted(range(1, n // 4), key=lambda z: -min(z, n // 4 - z))
    order = [z * 4 + low for low in (2, 3, 0, 1) for z in blocks] + [2, 3, 1]
    assert n % 4 == 0 and n & (n - 1) == 0 and sorted(order) == list(range(1, n))

    def each(order, function):
        for k in order:
            function(k)

    def rows_of(ref, lanes):
        return jnp.concatenate([ref[:, j, lanes] for j in range(hdev)], axis=0)

    barrier = pltpu.get_barrier_semaphore()
    each(
        order,
        lambda k: pl.semaphore_signal(
            barrier,
            inc=1,
            device_id={"hour": peer_of(k)},
            device_id_type=pl.DeviceIdType.MESH,
        ),
    )
    for i in (9, 0, 2, 7, 1, 5, 6, 8, 10, 11, 12, 13):
        loads[i].start()
    for i in first:
        loads[i].wait()
    for d in range(n):
        lanes = slice(d * ud, (d + 1) * ud)
        upper_stage[d] = rows_of(upper_in, lanes)
        lower_stage[d] = upper_stage[d] - rows_of(lower_in, lanes)
    pl.semaphore_wait(barrier, n - 1)

    each(order, lambda k: copy_to(lower_stage, lower, 1, peer_of(k)).start())
    each(order, lambda k: copy_to(upper_stage, upper, 0, peer_of(k)).start())
    upper[me] = upper_stage[me]
    lower[me] = lower_stage[me]
    for i in range(14):
        if i not in first and i != 7:
            loads[i].wait()
    for d in range(n):
        power[d] = rows_of(power_in, slice(d * ud, (d + 1) * ud))
    for j in range(hdev):
        flow[j * scen : (j + 1) * scen, :] = flow_in[:, j, :]
    piece = 128
    names = bus_in[...]
    for b in range(0, buses, piece):
        rows = lax.broadcasted_iota(jnp.int32, (piece, units), 0) + b
        inc[b : b + piece, :] = jnp.where(rows == names, 1.0, 0.0).astype(jnp.bfloat16)
    capacity_out[...] = capacity_in[...]
    retain = 1.0 - leak_in[pl.ds(me, 1), :]
    begin = start_in[pl.ds(me, 1), :]
    cost = cost_in[pl.ds(me, 1), :]
    eye = lax.broadcasted_iota(jnp.int32, (scen, scen), 0) == lax.broadcasted_iota(
        jnp.int32, (scen, scen), 1
    )
    price = jnp.concatenate(
        [
            jnp.sum(jnp.where(eye, price_in[j : j + 1, :], 0.0), axis=1, keepdims=True)
            for j in range(hdev)
        ],
        axis=0,
    )
    loads[7].wait()

    def place(t):
        return t // hdev, slice((t % hdev) * scen, (t % hdev + 1) * scen)

    def adjoint(difference):
        w = jnp.zeros((scen, ud), jnp.float32)
        for t in reversed(range(hours)):
            d, rows = place(t)
            w = retain * w + difference(d, rows)
            adj[d, rows, :] = w
        each(order, lambda k: copy_to(adj, adj_got, 2, peer_of(k)).start())
        adj_got[me] = adj[me]

    def iteration(first):
        bus_dual = jnp.dot(
            flow[...].astype(jnp.bfloat16), shift[...], preferred_element_type=jnp.float32
        ).astype(jnp.bfloat16)
        grid_grad = jnp.dot(bus_dual, inc[...], preferred_element_type=jnp.float32)
        for d in range(n):
            grid[d] = grid_grad[:, d * ud : (d + 1) * ud]

        def advance(d):
            limit = plimit_in[pl.ds(d, 1), :]
            old = power[d]
            trial = jnp.clip(
                old - primal_step * (grid[d] - adj_got[d] - price), -limit, limit
            )
            bar[d] = 2.0 * trial - old
            power[d] = trial

        advance(me)
        bar_got[me] = bar[me]

        def answer(k):
            source = peer_of(k)
            wait_from(adj_got, 2, source)
            advance(source)
            copy_to(bar, bar_got, 3, source).start()

        each(order, answer)
        for d in range(n):
            bar16[:, d * ud : (d + 1) * ud] = bar[d].astype(jnp.bfloat16)
        injection = lax.dot_general(
            bar16[...], inc[...], (((1,), (1,)), ((), ())), preferred_element_type=jnp.float32
        )
        load = jnp.concatenate([load_in[j] for j in range(hdev)], axis=0)
        injection = (injection - load.astype(jnp.float32)).astype(jnp.bfloat16)
        width = min(1024, lines)
        for c in range(0, lines, width):
            flows = lax.dot_general(
                injection,
                shift[c : c + width, :],
                (((1,), (1,)), ((), ())),
                preferred_element_type=jnp.float32,
            )
            probe = flow[:, c : c + width] + dual_step * flows
            edge = dual_step * limit_in[:, c : c + width]
            flow[:, c : c + width] = probe - jnp.clip(probe, -edge, edge)

        if first:

            def wait_upper(k):
                wait_from(upper, 0, peer_of(k))
                copy_to(upper_stage, upper, 0, peer_of(k)).wait_send()
                copy_to(lower_stage, lower, 1, peer_of(k)).wait_send()

            each(order, wait_upper)
            for d in range(n):
                lower[d] = upper[d] - lower[d]
        total = jnp.zeros((scen, ud), jnp.float32)
        for t in range(hours):
            d, rows = place(t)
            total = total + upper[d, rows, :]
        dual_total = jnp.sum(total, axis=0, keepdims=True)
        capacity = capacity_out[...]
        trial_capacity = jnp.maximum(
            capacity - primal_step * (hours * cost - dual_total / scen), 0.0
        )
        capacity_bar = 2.0 * trial_capacity - capacity
        capacity_out[...] = trial_capacity

        def wait_bar(k):
            wait_from(bar_got, 3, peer_of(k))
            copy_to(adj, adj_got, 2, peer_of(k)).wait_send()
            copy_to(bar, bar_got, 3, peer_of(k)).wait_send()

        each(order, wait_bar)
        e = jnp.broadcast_to(begin, (scen, ud))
        for t in range(hours):
            d, rows = place(t)
            e = retain * e - bar_got[d, rows, :]
            upper[d, rows, :] = jnp.maximum(
                upper[d, rows, :] + dual_step * (e - capacity_bar), 0.0
            )
            lower[d, rows, :] = jnp.maximum(lower[d, rows, :] - dual_step * e, 0.0)

    each(order, lambda k: wait_from(lower, 1, peer_of(k)))
    adjoint(lambda d, rows: lower[d, rows, :])
    iteration(True)

    def again(step, carry):
        adjoint(lambda d, rows: upper[d, rows, :] - lower[d, rows, :])
        iteration(False)
        return carry

    lax.fori_loop(1, ITERS, again, 0)

    def send_last(k):
        copy_to(upper, adj_got, 2, peer_of(k)).start()
        copy_to(lower, lower_stage, 0, peer_of(k)).start()

    each(order, send_last)
    adj_got[me] = upper[me]
    lower_stage[me] = lower[me]
    for d in range(n):
        for j in range(hdev):
            power_out[:, j, d * ud : (d + 1) * ud] = power[d, j * scen : (j + 1) * scen, :]
    for j in range(hdev):
        flow_out[:, j, :] = flow[j * scen : (j + 1) * scen, :]

    def wait_last(k):
        wait_from(adj_got, 2, peer_of(k))
        wait_from(lower_stage, 0, peer_of(k))
        copy_to(upper, adj_got, 2, peer_of(k)).wait_send()
        copy_to(lower, lower_stage, 0, peer_of(k)).wait_send()

    each(order, wait_last)
    for d in range(n):
        for j in range(hdev):
            lanes, rows = slice(d * ud, (d + 1) * ud), slice(j * scen, (j + 1) * scen)
            upper_out[:, j, lanes] = adj_got[d, rows, :]
            lower_out[:, j, lanes] = lower_stage[d, rows, :]


def store(*refs):
    sems = refs[10]
    copies = [
        pltpu.make_async_copy(refs[i], refs[5 + i], sems.at[i]) for i in (2, 0, 3, 4, 1)
    ]
    for copy in copies:
        copy.start()
    for copy in copies:
        copy.wait()


def kernel_rows(n, *refs):
    hbm, refs = refs[:14], refs[14:]
    (power_out, capacity_out, flow_out, upper_out, lower_out), refs = refs[:5], refs[5:]
    (
        capacity_in,
        flow_home,
        upper_home,
        price_in,
        load_in,
        shift,
        limit_in,
        bus_in,
        leak_in,
        start_in,
        plimit_in,
        cost_in,
        inc,
        inc_t,
        shift_t,
        upper,
        lower,
        power,
        flow_in,
        grid,
        bar,
        bar16,
        flow,
        flow2,
        flows1,
        first_src,
        first_dst,
        cap_src,
        cap_dst,
        grad_src,
        grad_dst,
        total_src,
        pair_dst,
        chip_src,
        total_dst,
        part_src,
        part_dst,
        last_src,
        last_dst,
        inj_src,
        inj_dst,
        state,
        mixed,
        adjoint,
        mixed_home,
        cap_ref,
        send_sems,
        recv_sems,
        pair_send,
        pair_recv,
        load_sems,
        own_sems,
    ) = refs
    me = lax.axis_index("hour")
    power_hbm, flow_hbm, upper_hbm, lower_hbm = hbm[0], hbm[2], hbm[3], hbm[4]
    hours = scen = n
    lines, buses = shift.shape
    ub, lb, bb = upper_home.shape[1], flow_home.shape[1], buses // 128
    quarter_lb = lb // 4
    units = ub * 128

    blocks = sorted(range(1, n // 4), key=lambda z: -min(z, n // 4 - z))
    order = [z * 4 + low for low in (2, 3, 0, 1) for z in blocks] + [2, 3, 1]
    assert n % 4 == 0 and n & (n - 1) == 0 and sorted(order) == list(range(1, n))

    barrier = pltpu.get_barrier_semaphore()
    for k in reversed(range(1, n)):
        pl.semaphore_signal(
            barrier,
            inc=1,
            device_id={"hour": me ^ k},
            device_id_type=pl.DeviceIdType.MESH,
        )
    loads = {}

    def load(name, src, dst, i):
        loads[name] = pltpu.make_async_copy(src, dst, load_sems.at[i])
        loads[name].start()

    load("upper", upper_hbm, upper_home, 0)
    load("price", hbm[5], price_in, 1)
    load("flow", flow_hbm, flow_home, 2)
    quarter = lines // 4
    for q in range(4):
        rows = pl.ds(q * quarter, quarter)
        load(("shift", q), hbm[7].at[rows], shift.at[rows], 3 + q)

    for i, (name, src, dst) in enumerate(
        (
            ("load", 6, load_in),
            ("bus", 9, bus_in),
            ("capacity", 1, capacity_in),
            ("cost", 13, cost_in),
            ("leak", 10, leak_in),
            ("plimit", 12, plimit_in),
            ("start", 11, start_in),
            ("limit", 8, limit_in),
        )
    ):
        load(name, hbm[src], dst, 7 + i)
    own = [
        pltpu.make_async_copy(src, dst.at[me], own_sems.at[i])
        for i, (src, dst) in enumerate(
            (
                (upper_hbm.at[me], upper),
                (lower_hbm.at[me], lower),
                (power_hbm.at[me], power),
            )
            + tuple(
                (flow_hbm.at[me, pl.ds(q * quarter_lb, quarter_lb)], flow_in.at[q])
                for q in range(4)
            )
        )
    ]
    for copy in own:
        copy.start()

    def push(source, dst, channel):
        for k in order:
            peer = me ^ k
            pltpu.make_async_remote_copy(
                src_ref=source(peer),
                dst_ref=dst.at[me],
                send_sem=send_sems.at[channel],
                recv_sem=recv_sems.at[channel],
                device_id={"hour": peer},
                device_id_type=pl.DeviceIdType.MESH,
            ).start()

    def everything(dst, channel):
        rest = dst.at[pl.ds(0, n - 1)]
        return pltpu.make_async_remote_copy(
            src_ref=rest,
            dst_ref=rest,
            send_sem=send_sems.at[channel],
            recv_sem=recv_sems.at[channel],
            device_id={"hour": me ^ 1},
            device_id_type=pl.DeviceIdType.MESH,
        )

    def arrive(dst, channel):
        everything(dst, channel).wait_recv()

    def lanes(j):
        return slice(j * 128, (j + 1) * 128)

    eye = lax.broadcasted_iota(jnp.int32, (scen, scen), 0) == lax.broadcasted_iota(
        jnp.int32, (scen, scen), 1
    )
    loads["upper"].wait()
    loads["price"].wait()
    part = upper_home[0]
    for s in range(1, scen):
        part = part + upper_home[s]
    price = jnp.sum(jnp.where(eye, price_in[...], 0.0), axis=1, keepdims=True)
    first_src[:, 0, :] = part
    first_src[:, 1, :] = jnp.broadcast_to(price, (scen, 128))
    pl.semaphore_wait(barrier, n - 1)

    push(lambda peer: first_src.at[peer], first_dst, 0)
    push(lambda peer: upper_hbm.at[peer], upper, 1)
    first_dst[me] = first_src[me]

    def bus_dual(rows):
        return jnp.dot(
            rows.astype(jnp.bfloat16), shift[...], preferred_element_type=jnp.float32
        ).astype(jnp.bfloat16)

    loads["flow"].wait()
    for j in range(lb):
        flow2[:, lanes(j)] = flow_home[:, j, :]
    for q in range(4):
        loads[("shift", q)].wait()
    dual = bus_dual(flow2[...]).astype(jnp.float32)
    loads["load"].wait()
    demand = load_in[0].astype(jnp.float32)
    for j in range(bb):
        grad_src[:, j, :] = dual[:, lanes(j)]
        grad_src[:, bb + j, :] = demand[:, lanes(j)]
    push(lambda peer: grad_src.at[peer], grad_dst, 4)
    push(lambda peer: lower_hbm.at[peer], lower, 2)
    grad_dst[me] = grad_src[me]

    loads["capacity"].wait()
    loads["cost"].wait()
    arrive(first_dst, 0)
    my_cost = cost_in[pl.ds(me, 1), :]

    def next_capacity(old, cost, total):
        return jnp.maximum(old - primal_step * (hours * cost - total / scen), 0.0)

    old = capacity_in[...]
    trial = next_capacity(old, my_cost, jnp.sum(first_dst[:, 0, :], axis=0, keepdims=True))
    cap_src[0:1, :] = trial
    cap_src[1:2, :] = 2.0 * trial - old
    push(lambda peer: cap_src, cap_dst, 5)
    cap_dst[me] = cap_src[...]
    push(lambda peer: power_hbm.at[peer], power, 3)

    for name in ("bus", "leak", "plimit", "start", "limit"):
        loads[name].wait()
    piece = 128
    names = bus_in[...]
    for b in range(0, buses, piece):
        rows = lax.broadcasted_iota(jnp.int32, (piece, units), 0) + b
        inc[b : b + piece, :] = jnp.where(rows == names, 1.0, 0.0).astype(jnp.bfloat16)
    retain = 1.0 - leak_in[...]
    plimit = plimit_in[...]
    for b in range(0, buses, piece):
        inc_t[:, b : b + piece] = inc[b : b + piece, :].T
    for c in range(0, lines, 512):
        shift_t[:, c : c + 512] = shift[c : c + 512, :].T
    width = min(1024, lines)

    def gradient(dual):
        value = jnp.dot(dual, inc[...], preferred_element_type=jnp.float32)
        for j in range(ub):
            grid[:, j, :] = value[:, lanes(j)]

    def adjoints():
        w = jnp.zeros((ub, 128), jnp.float32)
        for t in reversed(range(hours)):
            w = retain * w + (upper[t] - lower[t])
            adjoint[t] = w

    def primal(old_from, dual_from, prices, new_to):
        for t in range(hours):
            old = old_from[t]
            trial = jnp.clip(
                old - primal_step * (grid[t] - dual_from[t] - prices[t, 1:2, :]),
                -plimit,
                plimit,
            )
            bar[t] = 2.0 * trial - old
            if new_to is not None:
                new_to[t] = trial

    def states():
        e = start_in[...]
        for t in range(hours):
            e = retain * e - bar[t]
            state[t] = e

    def inject(i):
        for j in range(ub):
            bar16[:, lanes(j)] = bar[:, j, :].astype(jnp.bfloat16)
        value = jnp.dot(bar16[...], inc_t[...], preferred_element_type=jnp.float32)
        demand = jnp.concatenate([grad_dst[:, bb + j, :] for j in range(bb)], axis=1)
        value = (value - demand).astype(jnp.bfloat16)
        wide = value.astype(jnp.float32)
        for j in range(bb):
            inj_src[i, :, j, :] = wide[:, lanes(j)]
        return value

    def send_injection(i):
        push(lambda peer: inj_src.at[i, peer], inj_dst.at[i], (8, 9, 10, 14)[i])
        inj_dst[i, me] = inj_src[i, me]

    def injected(i):
        arrive(inj_dst.at[i], (8, 9, 10, 14)[i])
        return jnp.concatenate([inj_dst[i, :, j, :] for j in range(bb)], axis=1).astype(
            jnp.bfloat16
        )

    def line_flows(value, c):
        return jnp.dot(value, shift_t[:, c : c + width], preferred_element_type=jnp.float32)

    def advance(ref, c, flows):
        probe = ref[:, c : c + width] + dual_step * flows
        edge = dual_step * limit_in[:, c : c + width]
        ref[:, c : c + width] = probe - jnp.clip(probe, -edge, edge)

    def lines_step(ref, value):
        for c in range(0, lines, width):
            advance(ref, c, line_flows(value, c))

    def partial_dual(ref, c):
        return jnp.dot(
            ref[:, c : c + width].astype(jnp.bfloat16),
            shift[c : c + width, :],
            preferred_element_type=jnp.float32,
        )

    def flow_step(ref, value):
        dual = jnp.zeros((n, buses), jnp.float32)
        for c in range(0, lines, width):
            advance(ref, c, line_flows(value, c))
            dual = dual + partial_dual(ref, c)
        return dual.astype(jnp.bfloat16)

    def update_duals(capacity_bar):
        total = jnp.zeros((ub, 128), jnp.float32)
        for t in range(hours):
            e = state[t]
            raised = jnp.maximum(upper[t] + dual_step * (e - capacity_bar), 0.0)
            upper[t] = raised
            total = total + raised
            lower[t] = jnp.maximum(lower[t] - dual_step * e, 0.0)
        return total

    hb = ub // 2
    side = me % 2

    def pair_copy(i):
        return pltpu.make_async_remote_copy(
            src_ref=total_src.at[i, 1 - side],
            dst_ref=pair_dst.at[i],
            send_sem=pair_send.at[i],
            recv_sem=pair_recv.at[i],
            device_id={"hour": me ^ 1},
            device_id_type=pl.DeviceIdType.MESH,
        )

    def pair_up(i, total):
        total_src[i, 0] = total[:hb]
        total_src[i, 1] = total[hb:]
        pair_copy(i).start()

    def broadcast(i):
        pair_copy(i).wait_recv()
        chip = total_src[i, side] + pair_dst[i]
        chip_src[i] = chip
        push(lambda peer: chip_src.at[i], total_dst.at[i], 11 + i)
        total_dst[i, me] = chip

    def capacity_step(i):
        arrive(total_dst.at[i], 11 + i)
        low, high = total_dst[i, 0], total_dst[i, 1]
        for d in range(2, n, 2):
            low = low + total_dst[i, d]
            high = high + total_dst[i, d + 1]
        total = jnp.concatenate([low, high], axis=0)
        old = cap_ref[...]
        trial = next_capacity(old, cost_in[...], total)
        cap_ref[...] = trial
        return 2.0 * trial - old

    for copy in own:
        copy.wait()

    def push_flow(q):
        push(
            lambda peer: flow_hbm.at[peer, pl.ds(q * quarter_lb, quarter_lb)],
            flow_in.at[q],
            (6, 7, 19, 20)[q],
        )

    arrive(upper, 1)
    arrive(grad_dst, 4)
    push_flow(0)
    arrive(lower, 2)
    push_flow(1)
    push_flow(2)
    push_flow(3)
    arrive(power, 3)
    gradient(
        jnp.concatenate([grad_dst[:, j, :] for j in range(bb)], axis=1).astype(jnp.bfloat16)
    )
    adjoints()
    primal(power, adjoint, first_dst, power)
    states()
    arrive(cap_dst, 5)
    cap_ref[...] = cap_dst[:, 0, :]
    pair_up(0, update_duals(cap_dst[:, 1, :]))
    value = inject(0)
    broadcast(0)
    adjoints()
    for c in range(0, lines, width):
        flows1[:, c : c + width] = line_flows(value, c)
    dual = jnp.zeros((n, buses), jnp.float32)
    for q in range(4):
        arrive(flow_in.at[q], (6, 7, 19, 20)[q])
        for j in range(quarter_lb):
            flow[:, lanes(q * quarter_lb + j)] = flow_in[q, :, j, :]
        for c in range(q * quarter_lb * 128, (q + 1) * quarter_lb * 128, width):
            advance(flow, c, flows1[:, c : c + width])
            dual = dual + partial_dual(flow, c)

    gradient(dual.astype(jnp.bfloat16))
    primal(power, adjoint, first_dst, power)
    send_injection(0)
    states()
    pair_up(1, update_duals(capacity_step(0)))
    value = inject(1)
    broadcast(1)
    send_injection(1)
    adjoints()
    gradient(flow_step(flow, value))
    primal(power, adjoint, first_dst, power)
    states()
    part_src[:, 0, :] = update_duals(capacity_step(1))
    push(lambda peer: part_src.at[peer], part_dst, 13)
    part_dst[me] = part_src[me]
    adjoints()
    for t in range(hours):
        mixed[t] = power[t] + primal_step * adjoint[t]
    push(lambda peer: mixed.at[peer], mixed_home, 15)
    mixed_home[me] = mixed[me]
    value = inject(2)
    send_injection(2)
    gradient(flow_step(flow, value))
    primal(power, adjoint, first_dst, None)
    e = start_in[...]
    for t in range(hours):
        e = retain * e - bar[t]
        lower[t] = jnp.maximum(lower[t] - dual_step * e, 0.0)
        upper[t] = upper[t] + dual_step * e
    inject(3)
    send_injection(3)
    push(lambda peer: lower.at[peer], lower_out, 16)
    lower_out[me] = lower[me]
    upper_out[me] = upper[me]
    lines_step(flow2, injected(0))
    arrive(part_dst, 13)
    old = cap_ref[pl.ds(me, 1), :]
    trial = next_capacity(old, my_cost, jnp.sum(part_dst[:, 0, :], axis=0, keepdims=True))
    capacity_out[...] = trial
    last_src[...] = 2.0 * trial - old
    push(lambda peer: last_src, last_dst, 18)
    push(lambda peer: upper.at[peer], upper_out, 17)
    last_dst[me] = last_src[...]

    lines_step(flow2, injected(1))
    gradient(flow_step(flow2, injected(2)))
    arrive(mixed_home, 15)
    for s in range(scen):
        power_out[s] = jnp.clip(
            mixed_home[s] - primal_step * (grid[s] - first_src[s, 1:2, :]), -plimit, plimit
        )
    lines_step(flow2, injected(3))
    for j in range(lb):
        flow_out[:, j, :] = flow2[:, lanes(j)]
    arrive(lower_out, 16)
    arrive(upper_out, 17)
    arrive(last_dst, 18)
    raised = dual_step * last_dst[:, 0, :]
    for s in range(scen):
        upper_out[s] = jnp.maximum(upper_out[s] - raised, 0.0)
    sent = (
        [first_dst, upper, lower, power, grad_dst, cap_dst, flow_in.at[0], flow_in.at[1]]
        + [inj_dst.at[i] for i in range(3)]
        + [total_dst.at[i] for i in range(2)]
        + [part_dst, inj_dst.at[3], mixed_home, lower_out, upper_out, last_dst]
        + [flow_in.at[2], flow_in.at[3]]
    )
    for channel, dst in enumerate(sent):
        everything(dst, channel).wait_send()
    for i in range(2):
        pair_copy(i).wait_send()


def by_rows(n, args):
    power, capacity, flow, upper, lower, price, load, shift, limit, bus = args[:10]
    leak, start, plimit, cost = args[10:]
    scen, _, units = power.shape
    lines, buses = shift.shape
    ub, lb, bb = units // 128, lines // 128, buses // 128
    vmem = pl.BlockSpec(memory_space=pltpu.VMEM)
    hbm = pl.BlockSpec(memory_space=pltpu.HBM)
    state, wide = (scen, ub, 128), (scen, lb, 128)
    args = (
        power.reshape(state),
        capacity,
        flow.reshape(wide),
        upper.reshape(state),
        lower.reshape(state),
        price,
        load,
        shift,
        limit,
        bus,
        leak,
        start,
        plimit,
        cost,
    )
    f32 = jnp.float32
    results = tuple(jax.ShapeDtypeStruct(args[i].shape, f32) for i in range(5))

    def buffer(*shape, dtype=f32):
        return pltpu.VMEM(shape, dtype)

    out = pl.pallas_call(
        functools.partial(kernel_rows, n),
        out_shape=results,
        in_specs=[hbm] * 14,
        out_specs=(vmem,) * 5,
        scratch_shapes=[pltpu.VMEM(args[i].shape, args[i].dtype) for i in (1, 2, 3)]
        + [pltpu.VMEM(a.shape, a.dtype) for a in args[5:]]
        + [buffer(buses, units, dtype=jnp.bfloat16)]
        + [buffer(units, buses, dtype=jnp.bfloat16)]
        + [buffer(buses, lines, dtype=jnp.bfloat16)]
        + [buffer(*state)] * 3
        + [buffer(4, n, lb // 4, 128)]
        + [buffer(*state)] * 2
        + [buffer(n, units, dtype=jnp.bfloat16)]
        + [buffer(n, lines)] * 3
        + [
            buffer(n, 2, 128),
            buffer(n, 2, 128),
            buffer(2, 128),
            buffer(n, 2, 128),
            buffer(n, 2 * bb, 128),
            buffer(n, 2 * bb, 128),
            buffer(2, 2, ub // 2, 128),
            buffer(2, ub // 2, 128),
            buffer(2, ub // 2, 128),
            buffer(2, n, ub // 2, 128),
            buffer(n, 1, 128),
            buffer(n, 1, 128),
            buffer(1, 128),
            buffer(n, 1, 128),
            buffer(4, n, bb, 128),
            buffer(4, n, bb, 128),
            buffer(*state),
            buffer(*state),
            buffer(*state),
            buffer(*state),
            buffer(ub, 128),
            pltpu.SemaphoreType.DMA((21,)),
            pltpu.SemaphoreType.DMA((21,)),
            pltpu.SemaphoreType.DMA((2,)),
            pltpu.SemaphoreType.DMA((2,)),
            pltpu.SemaphoreType.DMA((15,)),
            pltpu.SemaphoreType.DMA((7,)),
        ],
        compiler_params=pltpu.CompilerParams(
            collective_id=0, has_side_effects=True, vmem_limit_bytes=48 * 1024 * 1024
        ),
    )(*(pltpu.with_memory_space_constraint(a, pltpu.HBM) for a in args))
    out = pl.pallas_call(
        store,
        out_shape=results,
        in_specs=[vmem] * 5,
        out_specs=(hbm,) * 5,
        scratch_shapes=[pltpu.SemaphoreType.DMA((5,))],
        compiler_params=pltpu.CompilerParams(vmem_limit_bytes=16 * 1024 * 1024),
    )(*out)
    return (
        out[0].reshape(power.shape),
        out[1].reshape(units // n),
        out[2].reshape(flow.shape),
        out[3].reshape(upper.shape),
        out[4].reshape(lower.shape),
    )


def on_device(
    power,
    capacity,
    flow_dual,
    upper_dual,
    lower_dual,
    price,
    load,
    shift_factors,
    line_limit,
    unit_bus,
    leakage,
    initial_state,
    power_limit,
    capacity_cost,
):
    n = lax.axis_size("hour")
    scen, hdev, units = power.shape
    lines, buses = shift_factors.shape
    ud, rows = units // n, scen * hdev
    block = pltpu.VMEM((n, rows, ud), jnp.float32)
    vmem = pl.BlockSpec(memory_space=pltpu.VMEM)
    hbm = pl.BlockSpec(memory_space=pltpu.HBM)
    args = (
        power,
        capacity.reshape(1, ud),
        flow_dual,
        upper_dual,
        lower_dual,
        price.T,
        load.transpose(1, 0, 2),
        shift_factors,
        line_limit.reshape(1, lines),
        unit_bus.reshape(1, units),
        leakage.reshape(n, ud),
        initial_state.reshape(n, ud),
        power_limit.reshape(n, ud),
        capacity_cost.reshape(n, ud),
    )
    if scen == n and hdev == 1 and ud == 128 and lines % 1024 == 0 and buses % 128 == 0:
        return by_rows(n, args)
    results = tuple(
        jax.ShapeDtypeStruct(args[i].shape, jnp.float32) for i in range(5)
    )
    out = pl.pallas_call(
        functools.partial(kernel, n),
        out_shape=results,
        in_specs=[hbm] * 14,
        out_specs=(vmem,) * 5,
        scratch_shapes=[pltpu.VMEM(a.shape, a.dtype) for a in args]
        + [
            pltpu.VMEM((buses, units), jnp.bfloat16),
            block,
            block,
            pltpu.VMEM((rows, lines), jnp.float32),
            pltpu.VMEM((rows, units), jnp.bfloat16),
        ]
        + [block] * 8
        + [
            pltpu.SemaphoreType.DMA((4, n)),
            pltpu.SemaphoreType.DMA((4, n)),
            pltpu.SemaphoreType.DMA((14,)),
        ],
        compiler_params=pltpu.CompilerParams(
            collective_id=0, has_side_effects=True, vmem_limit_bytes=48 * 1024 * 1024
        ),
    )(*(pltpu.with_memory_space_constraint(a, pltpu.HBM) for a in args))
    out = pl.pallas_call(
        store,
        out_shape=results,
        in_specs=[vmem] * 5,
        out_specs=(hbm,) * 5,
        scratch_shapes=[pltpu.SemaphoreType.DMA((5,))],
        compiler_params=pltpu.CompilerParams(vmem_limit_bytes=16 * 1024 * 1024),
    )(*out)
    return (out[0], out[1].reshape(ud), out[2], out[3], out[4])


def solution(mesh):
    return jax.shard_map(
        on_device,
        mesh=mesh,
        in_specs=(
            P("groups", "hour", None),
            P(("groups", "hour")),
            P("groups", "hour", None),
            P("groups", "hour", None),
            P("groups", "hour", None),
            P("groups", "hour"),
            P("groups", "hour", None),
            P(),
            P(),
            P(),
            P(),
            P("groups"),
            P(),
            P(),
        ),
        out_specs=(
            P("groups", "hour", None),
            P(("groups", "hour")),
            P("groups", "hour", None),
            P("groups", "hour", None),
            P("groups", "hour", None),
        ),
        check_vma=False,
    )
```

```python
import functools

import jax
import jax.numpy as jnp
from jax import lax
from jax.experimental import pallas as pl
from jax.experimental.pallas import tpu as pltpu
from jax.sharding import PartitionSpec as P

ITERS = 4

primal_step = 0.05
dual_step = 0.01


def kernel(n, *refs):
    arrived, refs = refs[:14], refs[14:]
    (power_out, capacity_out, flow_out, upper_out, lower_out), refs = refs[:5], refs[5:]
    held, refs = refs[:14], refs[14:]
    (
        power_in,
        capacity_in,
        flow_in,
        upper_in,
        lower_in,
        price_in,
        load_in,
        shift,
        limit_in,
        bus_in,
        leak_in,
        start_in,
        plimit_in,
        cost_in,
    ) = held
    (
        inc,
        power,
        grid,
        flow,
        bar16,
        upper,
        lower,
        upper_stage,
        lower_stage,
        adj,
        adj_got,
        bar,
        bar_got,
        send_sems,
        recv_sems,
        load_sems,
    ) = refs
    me = lax.axis_index("hour")
    scen, hdev, units = power_in.shape
    lines, buses = shift.shape
    ud = units // n
    hours = hdev * n
    loads = [
        pltpu.make_async_copy(src, dst, load_sems.at[i])
        for i, (src, dst) in enumerate(zip(arrived, held))
    ]
    first = (3, 4)
    for i in first:
        loads[i].start()

    def peer_of(k):
        return me ^ k

    def copy_to(src, dst, channel, peer):
        return pltpu.make_async_remote_copy(
            src_ref=src.at[peer],
            dst_ref=dst.at[me],
            send_sem=send_sems.at[channel, peer],
            recv_sem=recv_sems.at[channel, me],
            device_id={"hour": peer},
            device_id_type=pl.DeviceIdType.MESH,
        )

    def wait_from(dst, channel, source):
        pltpu.make_async_remote_copy(
            src_ref=dst.at[source],
            dst_ref=dst.at[source],
            send_sem=send_sems.at[channel, source],
            recv_sem=recv_sems.at[channel, source],
            device_id={"hour": source},
            device_id_type=pl.DeviceIdType.MESH,
        ).wait_recv()

    blocks = sorted(range(1, n // 4), key=lambda z: -min(z, n // 4 - z))
    order = [z * 4 + low for low in (2, 3, 0, 1) for z in blocks] + [2, 3, 1]
    assert n % 4 == 0 and n & (n - 1) == 0 and sorted(order) == list(range(1, n))

    def each(order, function):
        for k in order:
            function(k)

    def rows_of(ref, lanes):
        return jnp.concatenate([ref[:, j, lanes] for j in range(hdev)], axis=0)

    barrier = pltpu.get_barrier_semaphore()
    each(
        order,
        lambda k: pl.semaphore_signal(
            barrier,
            inc=1,
            device_id={"hour": peer_of(k)},
            device_id_type=pl.DeviceIdType.MESH,
        ),
    )
    for i in (9, 0, 2, 7, 1, 5, 6, 8, 10, 11, 12, 13):
        loads[i].start()
    for i in first:
        loads[i].wait()
    for d in range(n):
        lanes = slice(d * ud, (d + 1) * ud)
        upper_stage[d] = rows_of(upper_in, lanes)
        lower_stage[d] = upper_stage[d] - rows_of(lower_in, lanes)
    pl.semaphore_wait(barrier, n - 1)

    each(order, lambda k: copy_to(lower_stage, lower, 1, peer_of(k)).start())
    each(order, lambda k: copy_to(upper_stage, upper, 0, peer_of(k)).start())
    upper[me] = upper_stage[me]
    lower[me] = lower_stage[me]
    for i in range(14):
        if i not in first and i != 7:
            loads[i].wait()
    for d in range(n):
        power[d] = rows_of(power_in, slice(d * ud, (d + 1) * ud))
    for j in range(hdev):
        flow[j * scen : (j + 1) * scen, :] = flow_in[:, j, :]
    piece = 128
    names = bus_in[...]
    for b in range(0, buses, piece):
        rows = lax.broadcasted_iota(jnp.int32, (piece, units), 0) + b
        inc[b : b + piece, :] = jnp.where(rows == names, 1.0, 0.0).astype(jnp.bfloat16)
    capacity_out[...] = capacity_in[...]
    retain = 1.0 - leak_in[pl.ds(me, 1), :]
    begin = start_in[pl.ds(me, 1), :]
    cost = cost_in[pl.ds(me, 1), :]
    eye = lax.broadcasted_iota(jnp.int32, (scen, scen), 0) == lax.broadcasted_iota(
        jnp.int32, (scen, scen), 1
    )
    price = jnp.concatenate(
        [
            jnp.sum(jnp.where(eye, price_in[j : j + 1, :], 0.0), axis=1, keepdims=True)
            for j in range(hdev)
        ],
        axis=0,
    )
    loads[7].wait()

    def place(t):
        return t // hdev, slice((t % hdev) * scen, (t % hdev + 1) * scen)

    def adjoint(difference):
        w = jnp.zeros((scen, ud), jnp.float32)
        for t in reversed(range(hours)):
            d, rows = place(t)
            w = retain * w + difference(d, rows)
            adj[d, rows, :] = w
        each(order, lambda k: copy_to(adj, adj_got, 2, peer_of(k)).start())
        adj_got[me] = adj[me]

    def iteration(first):
        bus_dual = jnp.dot(
            flow[...].astype(jnp.bfloat16), shift[...], preferred_element_type=jnp.float32
        ).astype(jnp.bfloat16)
        grid_grad = jnp.dot(bus_dual, inc[...], preferred_element_type=jnp.float32)
        for d in range(n):
            grid[d] = grid_grad[:, d * ud : (d + 1) * ud]

        def advance(d):
            limit = plimit_in[pl.ds(d, 1), :]
            old = power[d]
            trial = jnp.clip(
                old - primal_step * (grid[d] - adj_got[d] - price), -limit, limit
            )
            bar[d] = 2.0 * trial - old
            power[d] = trial

        advance(me)
        bar_got[me] = bar[me]

        def answer(k):
            source = peer_of(k)
            wait_from(adj_got, 2, source)
            advance(source)
            copy_to(bar, bar_got, 3, source).start()

        each(order, answer)
        for d in range(n):
            bar16[:, d * ud : (d + 1) * ud] = bar[d].astype(jnp.bfloat16)
        injection = lax.dot_general(
            bar16[...], inc[...], (((1,), (1,)), ((), ())), preferred_element_type=jnp.float32
        )
        load = jnp.concatenate([load_in[j] for j in range(hdev)], axis=0)
        injection = (injection - load.astype(jnp.float32)).astype(jnp.bfloat16)
        width = min(1024, lines)
        for c in range(0, lines, width):
            flows = lax.dot_general(
                injection,
                shift[c : c + width, :],
                (((1,), (1,)), ((), ())),
                preferred_element_type=jnp.float32,
            )
            probe = flow[:, c : c + width] + dual_step * flows
            edge = dual_step * limit_in[:, c : c + width]
            flow[:, c : c + width] = probe - jnp.clip(probe, -edge, edge)

        if first:

            def wait_upper(k):
                wait_from(upper, 0, peer_of(k))
                copy_to(upper_stage, upper, 0, peer_of(k)).wait_send()
                copy_to(lower_stage, lower, 1, peer_of(k)).wait_send()

            each(order, wait_upper)
            for d in range(n):
                lower[d] = upper[d] - lower[d]
        total = jnp.zeros((scen, ud), jnp.float32)
        for t in range(hours):
            d, rows = place(t)
            total = total + upper[d, rows, :]
        dual_total = jnp.sum(total, axis=0, keepdims=True)
        capacity = capacity_out[...]
        trial_capacity = jnp.maximum(
            capacity - primal_step * (hours * cost - dual_total / scen), 0.0
        )
        capacity_bar = 2.0 * trial_capacity - capacity
        capacity_out[...] = trial_capacity

        def wait_bar(k):
            wait_from(bar_got, 3, peer_of(k))
            copy_to(adj, adj_got, 2, peer_of(k)).wait_send()
            copy_to(bar, bar_got, 3, peer_of(k)).wait_send()

        each(order, wait_bar)
        e = jnp.broadcast_to(begin, (scen, ud))
        for t in range(hours):
            d, rows = place(t)
            e = retain * e - bar_got[d, rows, :]
            upper[d, rows, :] = jnp.maximum(
                upper[d, rows, :] + dual_step * (e - capacity_bar), 0.0
            )
            lower[d, rows, :] = jnp.maximum(lower[d, rows, :] - dual_step * e, 0.0)

    each(order, lambda k: wait_from(lower, 1, peer_of(k)))
    adjoint(lambda d, rows: lower[d, rows, :])
    iteration(True)

    def again(step, carry):
        adjoint(lambda d, rows: upper[d, rows, :] - lower[d, rows, :])
        iteration(False)
        return carry

    lax.fori_loop(1, ITERS, again, 0)

    def send_last(k):
        copy_to(upper, adj_got, 2, peer_of(k)).start()
        copy_to(lower, lower_stage, 0, peer_of(k)).start()

    each(order, send_last)
    adj_got[me] = upper[me]
    lower_stage[me] = lower[me]
    for d in range(n):
        for j in range(hdev):
            power_out[:, j, d * ud : (d + 1) * ud] = power[d, j * scen : (j + 1) * scen, :]
    for j in range(hdev):
        flow_out[:, j, :] = flow[j * scen : (j + 1) * scen, :]

    def wait_last(k):
        wait_from(adj_got, 2, peer_of(k))
        wait_from(lower_stage, 0, peer_of(k))
        copy_to(upper, adj_got, 2, peer_of(k)).wait_send()
        copy_to(lower, lower_stage, 0, peer_of(k)).wait_send()

    each(order, wait_last)
    for d in range(n):
        for j in range(hdev):
            lanes, rows = slice(d * ud, (d + 1) * ud), slice(j * scen, (j + 1) * scen)
            upper_out[:, j, lanes] = adj_got[d, rows, :]
            lower_out[:, j, lanes] = lower_stage[d, rows, :]


def store(*refs):
    sems = refs[10]
    copies = [
        pltpu.make_async_copy(refs[i], refs[5 + i], sems.at[i]) for i in (2, 0, 3, 4, 1)
    ]
    for copy in copies:
        copy.start()
    for copy in copies:
        copy.wait()


def kernel_rows(n, *refs):
    hbm, refs = refs[:14], refs[14:]
    (power_out, capacity_out, flow_out, upper_out, lower_out), refs = refs[:5], refs[5:]
    (
        capacity_in,
        flow_home,
        upper_home,
        price_in,
        load_in,
        shift,
        limit_in,
        bus_in,
        leak_in,
        start_in,
        plimit_in,
        cost_in,
        inc,
        inc_t,
        shift_t,
        upper,
        lower,
        power,
        flow_in,
        grid,
        bar,
        bar16,
        flow,
        flow2,
        flows1,
        first_src,
        first_dst,
        cap_src,
        cap_dst,
        grad_src,
        grad_dst,
        total_src,
        pair_dst,
        chip_src,
        total_dst,
        part_src,
        part_dst,
        last_src,
        last_dst,
        inj_src,
        inj_dst,
        state,
        mixed,
        adjoint,
        mixed_home,
        cap_ref,
        send_sems,
        recv_sems,
        pair_send,
        pair_recv,
        load_sems,
        own_sems,
    ) = refs
    me = lax.axis_index("hour")
    power_hbm, flow_hbm, upper_hbm, lower_hbm = hbm[0], hbm[2], hbm[3], hbm[4]
    hours = scen = n
    lines, buses = shift.shape
    ub, lb, bb = upper_home.shape[1], flow_home.shape[1], buses // 128
    quarter_lb = lb // 4
    units = ub * 128

    blocks = sorted(range(1, n // 4), key=lambda z: -min(z, n // 4 - z))
    order = [z * 4 + low for low in (2, 3, 0, 1) for z in blocks] + [2, 3, 1]
    assert n % 4 == 0 and n & (n - 1) == 0 and sorted(order) == list(range(1, n))

    barrier = pltpu.get_barrier_semaphore()
    for k in reversed(range(1, n)):
        pl.semaphore_signal(
            barrier,
            inc=1,
            device_id={"hour": me ^ k},
            device_id_type=pl.DeviceIdType.MESH,
        )
    loads = {}

    def load(name, src, dst, i):
        loads[name] = pltpu.make_async_copy(src, dst, load_sems.at[i])
        loads[name].start()

    load("upper", upper_hbm, upper_home, 0)
    load("price", hbm[5], price_in, 1)
    load("flow", flow_hbm, flow_home, 2)
    quarter = lines // 4
    for q in range(4):
        rows = pl.ds(q * quarter, quarter)
        load(("shift", q), hbm[7].at[rows], shift.at[rows], 3 + q)

    for i, (name, src, dst) in enumerate(
        (
            ("load", 6, load_in),
            ("bus", 9, bus_in),
            ("capacity", 1, capacity_in),
            ("cost", 13, cost_in),
            ("leak", 10, leak_in),
            ("plimit", 12, plimit_in),
            ("start", 11, start_in),
            ("limit", 8, limit_in),
        )
    ):
        load(name, hbm[src], dst, 7 + i)
    own = [
        pltpu.make_async_copy(src, dst.at[me], own_sems.at[i])
        for i, (src, dst) in enumerate(
            (
                (upper_hbm.at[me], upper),
                (lower_hbm.at[me], lower),
                (power_hbm.at[me], power),
            )
            + tuple(
                (flow_hbm.at[me, pl.ds(q * quarter_lb, quarter_lb)], flow_in.at[q])
                for q in range(4)
            )
        )
    ]
    for copy in own:
        copy.start()

    def push(source, dst, channel):
        for k in order:
            peer = me ^ k
            pltpu.make_async_remote_copy(
                src_ref=source(peer),
                dst_ref=dst.at[me],
                send_sem=send_sems.at[channel],
                recv_sem=recv_sems.at[channel],
                device_id={"hour": peer},
                device_id_type=pl.DeviceIdType.MESH,
            ).start()

    def everything(dst, channel):
        rest = dst.at[pl.ds(0, n - 1)]
        return pltpu.make_async_remote_copy(
            src_ref=rest,
            dst_ref=rest,
            send_sem=send_sems.at[channel],
            recv_sem=recv_sems.at[channel],
            device_id={"hour": me ^ 1},
            device_id_type=pl.DeviceIdType.MESH,
        )

    def arrive(dst, channel):
        everything(dst, channel).wait_recv()

    def lanes(j):
        return slice(j * 128, (j + 1) * 128)

    eye = lax.broadcasted_iota(jnp.int32, (scen, scen), 0) == lax.broadcasted_iota(
        jnp.int32, (scen, scen), 1
    )
    loads["upper"].wait()
    loads["price"].wait()
    part = upper_home[0]
    for s in range(1, scen):
        part = part + upper_home[s]
    price = jnp.sum(jnp.where(eye, price_in[...], 0.0), axis=1, keepdims=True)
    first_src[:, 0, :] = part
    first_src[:, 1, :] = jnp.broadcast_to(price, (scen, 128))
    pl.semaphore_wait(barrier, n - 1)

    push(lambda peer: first_src.at[peer], first_dst, 0)
    push(lambda peer: upper_hbm.at[peer], upper, 1)
    first_dst[me] = first_src[me]

    def bus_dual(rows):
        return jnp.dot(
            rows.astype(jnp.bfloat16), shift[...], preferred_element_type=jnp.float32
        ).astype(jnp.bfloat16)

    loads["flow"].wait()
    for j in range(lb):
        flow2[:, lanes(j)] = flow_home[:, j, :]
    for q in range(4):
        loads[("shift", q)].wait()
    dual = bus_dual(flow2[...]).astype(jnp.float32)
    loads["load"].wait()
    demand = load_in[0].astype(jnp.float32)
    for j in range(bb):
        grad_src[:, j, :] = dual[:, lanes(j)]
        grad_src[:, bb + j, :] = demand[:, lanes(j)]
    push(lambda peer: grad_src.at[peer], grad_dst, 4)
    push(lambda peer: lower_hbm.at[peer], lower, 2)
    grad_dst[me] = grad_src[me]

    loads["capacity"].wait()
    loads["cost"].wait()
    arrive(first_dst, 0)
    my_cost = cost_in[pl.ds(me, 1), :]

    def next_capacity(old, cost, total):
        return jnp.maximum(old - primal_step * (hours * cost - total / scen), 0.0)

    old = capacity_in[...]
    trial = next_capacity(old, my_cost, jnp.sum(first_dst[:, 0, :], axis=0, keepdims=True))
    cap_src[0:1, :] = trial
    cap_src[1:2, :] = 2.0 * trial - old
    push(lambda peer: cap_src, cap_dst, 5)
    cap_dst[me] = cap_src[...]
    push(lambda peer: power_hbm.at[peer], power, 3)

    for name in ("bus", "leak", "plimit", "start", "limit"):
        loads[name].wait()
    piece = 128
    names = bus_in[...]
    for b in range(0, buses, piece):
        rows = lax.broadcasted_iota(jnp.int32, (piece, units), 0) + b
        inc[b : b + piece, :] = jnp.where(rows == names, 1.0, 0.0).astype(jnp.bfloat16)
    retain = 1.0 - leak_in[...]
    plimit = plimit_in[...]
    for b in range(0, buses, piece):
        inc_t[:, b : b + piece] = inc[b : b + piece, :].T
    for c in range(0, lines, 512):
        shift_t[:, c : c + 512] = shift[c : c + 512, :].T
    width = min(1024, lines)

    def gradient(dual):
        value = jnp.dot(dual, inc[...], preferred_element_type=jnp.float32)
        for j in range(ub):
            grid[:, j, :] = value[:, lanes(j)]

    def adjoints():
        w = jnp.zeros((ub, 128), jnp.float32)
        for t in reversed(range(hours)):
            w = retain * w + (upper[t] - lower[t])
            adjoint[t] = w

    def primal(old_from, dual_from, prices, new_to):
        for t in range(hours):
            old = old_from[t]
            trial = jnp.clip(
                old - primal_step * (grid[t] - dual_from[t] - prices[t, 1:2, :]),
                -plimit,
                plimit,
            )
            bar[t] = 2.0 * trial - old
            if new_to is not None:
                new_to[t] = trial

    def states():
        e = start_in[...]
        for t in range(hours):
            e = retain * e - bar[t]
            state[t] = e

    def inject(i):
        for j in range(ub):
            bar16[:, lanes(j)] = bar[:, j, :].astype(jnp.bfloat16)
        value = jnp.dot(bar16[...], inc_t[...], preferred_element_type=jnp.float32)
        demand = jnp.concatenate([grad_dst[:, bb + j, :] for j in range(bb)], axis=1)
        value = (value - demand).astype(jnp.bfloat16)
        wide = value.astype(jnp.float32)
        for j in range(bb):
            inj_src[i, :, j, :] = wide[:, lanes(j)]
        return value

    def send_injection(i):
        push(lambda peer: inj_src.at[i, peer], inj_dst.at[i], (8, 9, 10, 14)[i])
        inj_dst[i, me] = inj_src[i, me]

    def injected(i):
        arrive(inj_dst.at[i], (8, 9, 10, 14)[i])
        return jnp.concatenate([inj_dst[i, :, j, :] for j in range(bb)], axis=1).astype(
            jnp.bfloat16
        )

    def line_flows(value, c):
        return jnp.dot(value, shift_t[:, c : c + width], preferred_element_type=jnp.float32)

    def advance(ref, c, flows):
        probe = ref[:, c : c + width] + dual_step * flows
        edge = dual_step * limit_in[:, c : c + width]
        ref[:, c : c + width] = probe - jnp.clip(probe, -edge, edge)

    def lines_step(ref, value):
        for c in range(0, lines, width):
            advance(ref, c, line_flows(value, c))

    def partial_dual(ref, c):
        return jnp.dot(
            ref[:, c : c + width].astype(jnp.bfloat16),
            shift[c : c + width, :],
            preferred_element_type=jnp.float32,
        )

    def flow_step(ref, value):
        dual = jnp.zeros((n, buses), jnp.float32)
        for c in range(0, lines, width):
            advance(ref, c, line_flows(value, c))
            dual = dual + partial_dual(ref, c)
        return dual.astype(jnp.bfloat16)

    def update_duals(capacity_bar):
        total = jnp.zeros((ub, 128), jnp.float32)
        for t in range(hours):
            e = state[t]
            raised = jnp.maximum(upper[t] + dual_step * (e - capacity_bar), 0.0)
            upper[t] = raised
            total = total + raised
            lower[t] = jnp.maximum(lower[t] - dual_step * e, 0.0)
        return total

    hb = ub // 2
    side = me % 2

    def pair_copy(i):
        return pltpu.make_async_remote_copy(
            src_ref=total_src.at[i, 1 - side],
            dst_ref=pair_dst.at[i],
            send_sem=pair_send.at[i],
            recv_sem=pair_recv.at[i],
            device_id={"hour": me ^ 1},
            device_id_type=pl.DeviceIdType.MESH,
        )

    def pair_up(i, total):
        total_src[i, 0] = total[:hb]
        total_src[i, 1] = total[hb:]
        pair_copy(i).start()

    def broadcast(i):
        pair_copy(i).wait_recv()
        chip = total_src[i, side] + pair_dst[i]
        chip_src[i] = chip
        push(lambda peer: chip_src.at[i], total_dst.at[i], 11 + i)
        total_dst[i, me] = chip

    def capacity_step(i):
        arrive(total_dst.at[i], 11 + i)
        low, high = total_dst[i, 0], total_dst[i, 1]
        for d in range(2, n, 2):
            low = low + total_dst[i, d]
            high = high + total_dst[i, d + 1]
        total = jnp.concatenate([low, high], axis=0)
        old = cap_ref[...]
        trial = next_capacity(old, cost_in[...], total)
        cap_ref[...] = trial
        return 2.0 * trial - old

    for copy in own:
        copy.wait()

    def push_flow(q):
        push(
            lambda peer: flow_hbm.at[peer, pl.ds(q * quarter_lb, quarter_lb)],
            flow_in.at[q],
            (6, 7, 19, 20)[q],
        )

    arrive(upper, 1)
    arrive(grad_dst, 4)
    push_flow(0)
    arrive(lower, 2)
    push_flow(1)
    push_flow(2)
    push_flow(3)
    arrive(power, 3)
    gradient(
        jnp.concatenate([grad_dst[:, j, :] for j in range(bb)], axis=1).astype(jnp.bfloat16)
    )
    adjoints()
    primal(power, adjoint, first_dst, power)
    states()
    arrive(cap_dst, 5)
    cap_ref[...] = cap_dst[:, 0, :]
    pair_up(0, update_duals(cap_dst[:, 1, :]))
    value = inject(0)
    broadcast(0)
    adjoints()
    for c in range(0, lines, width):
        flows1[:, c : c + width] = line_flows(value, c)
    dual = jnp.zeros((n, buses), jnp.float32)
    for q in range(4):
        arrive(flow_in.at[q], (6, 7, 19, 20)[q])
        for j in range(quarter_lb):
            flow[:, lanes(q * quarter_lb + j)] = flow_in[q, :, j, :]
        for c in range(q * quarter_lb * 128, (q + 1) * quarter_lb * 128, width):
            advance(flow, c, flows1[:, c : c + width])
            dual = dual + partial_dual(flow, c)

    gradient(dual.astype(jnp.bfloat16))
    primal(power, adjoint, first_dst, power)
    send_injection(0)
    states()
    pair_up(1, update_duals(capacity_step(0)))
    value = inject(1)
    broadcast(1)
    send_injection(1)
    adjoints()
    gradient(flow_step(flow, value))
    primal(power, adjoint, first_dst, power)
    states()
    value = inject(2)
    send_injection(2)
    part_src[:, 0, :] = update_duals(capacity_step(1))
    push(lambda peer: part_src.at[peer], part_dst, 13)
    part_dst[me] = part_src[me]
    adjoints()
    for t in range(hours):
        mixed[t] = power[t] + primal_step * adjoint[t]
    push(lambda peer: mixed.at[peer], mixed_home, 15)
    mixed_home[me] = mixed[me]
    gradient(flow_step(flow, value))
    primal(power, adjoint, first_dst, None)
    e = start_in[...]
    for t in range(hours):
        e = retain * e - bar[t]
        lower[t] = jnp.maximum(lower[t] - dual_step * e, 0.0)
        upper[t] = upper[t] + dual_step * e
    inject(3)
    send_injection(3)
    push(lambda peer: lower.at[peer], lower_out, 16)
    lower_out[me] = lower[me]
    upper_out[me] = upper[me]
    lines_step(flow2, injected(0))
    arrive(part_dst, 13)
    old = cap_ref[pl.ds(me, 1), :]
    trial = next_capacity(old, my_cost, jnp.sum(part_dst[:, 0, :], axis=0, keepdims=True))
    capacity_out[...] = trial
    last_src[...] = 2.0 * trial - old
    push(lambda peer: last_src, last_dst, 18)
    push(lambda peer: upper.at[peer], upper_out, 17)
    last_dst[me] = last_src[...]

    lines_step(flow2, injected(1))
    gradient(flow_step(flow2, injected(2)))
    arrive(mixed_home, 15)
    for s in range(scen):
        power_out[s] = jnp.clip(
            mixed_home[s] - primal_step * (grid[s] - first_src[s, 1:2, :]), -plimit, plimit
        )
    lines_step(flow2, injected(3))
    for j in range(lb):
        flow_out[:, j, :] = flow2[:, lanes(j)]
    arrive(lower_out, 16)
    arrive(upper_out, 17)
    arrive(last_dst, 18)
    raised = dual_step * last_dst[:, 0, :]
    for s in range(scen):
        upper_out[s] = jnp.maximum(upper_out[s] - raised, 0.0)
    sent = (
        [first_dst, upper, lower, power, grad_dst, cap_dst, flow_in.at[0], flow_in.at[1]]
        + [inj_dst.at[i] for i in range(3)]
        + [total_dst.at[i] for i in range(2)]
        + [part_dst, inj_dst.at[3], mixed_home, lower_out, upper_out, last_dst]
        + [flow_in.at[2], flow_in.at[3]]
    )
    for channel, dst in enumerate(sent):
        everything(dst, channel).wait_send()
    for i in range(2):
        pair_copy(i).wait_send()


def by_rows(n, args):
    power, capacity, flow, upper, lower, price, load, shift, limit, bus = args[:10]
    leak, start, plimit, cost = args[10:]
    scen, _, units = power.shape
    lines, buses = shift.shape
    ub, lb, bb = units // 128, lines // 128, buses // 128
    vmem = pl.BlockSpec(memory_space=pltpu.VMEM)
    hbm = pl.BlockSpec(memory_space=pltpu.HBM)
    state, wide = (scen, ub, 128), (scen, lb, 128)
    args = (
        power.reshape(state),
        capacity,
        flow.reshape(wide),
        upper.reshape(state),
        lower.reshape(state),
        price,
        load,
        shift,
        limit,
        bus,
        leak,
        start,
        plimit,
        cost,
    )
    f32 = jnp.float32
    results = tuple(jax.ShapeDtypeStruct(args[i].shape, f32) for i in range(5))

    def buffer(*shape, dtype=f32):
        return pltpu.VMEM(shape, dtype)

    out = pl.pallas_call(
        functools.partial(kernel_rows, n),
        out_shape=results,
        in_specs=[hbm] * 14,
        out_specs=(vmem,) * 5,
        scratch_shapes=[pltpu.VMEM(args[i].shape, args[i].dtype) for i in (1, 2, 3)]
        + [pltpu.VMEM(a.shape, a.dtype) for a in args[5:]]
        + [buffer(buses, units, dtype=jnp.bfloat16)]
        + [buffer(units, buses, dtype=jnp.bfloat16)]
        + [buffer(buses, lines, dtype=jnp.bfloat16)]
        + [buffer(*state)] * 3
        + [buffer(4, n, lb // 4, 128)]
        + [buffer(*state)] * 2
        + [buffer(n, units, dtype=jnp.bfloat16)]
        + [buffer(n, lines)] * 3
        + [
            buffer(n, 2, 128),
            buffer(n, 2, 128),
            buffer(2, 128),
            buffer(n, 2, 128),
            buffer(n, 2 * bb, 128),
            buffer(n, 2 * bb, 128),
            buffer(2, 2, ub // 2, 128),
            buffer(2, ub // 2, 128),
            buffer(2, ub // 2, 128),
            buffer(2, n, ub // 2, 128),
            buffer(n, 1, 128),
            buffer(n, 1, 128),
            buffer(1, 128),
            buffer(n, 1, 128),
            buffer(4, n, bb, 128),
            buffer(4, n, bb, 128),
            buffer(*state),
            buffer(*state),
            buffer(*state),
            buffer(*state),
            buffer(ub, 128),
            pltpu.SemaphoreType.DMA((21,)),
            pltpu.SemaphoreType.DMA((21,)),
            pltpu.SemaphoreType.DMA((2,)),
            pltpu.SemaphoreType.DMA((2,)),
            pltpu.SemaphoreType.DMA((15,)),
            pltpu.SemaphoreType.DMA((7,)),
        ],
        compiler_params=pltpu.CompilerParams(
            collective_id=0, has_side_effects=True, vmem_limit_bytes=48 * 1024 * 1024
        ),
    )(*(pltpu.with_memory_space_constraint(a, pltpu.HBM) for a in args))
    out = pl.pallas_call(
        store,
        out_shape=results,
        in_specs=[vmem] * 5,
        out_specs=(hbm,) * 5,
        scratch_shapes=[pltpu.SemaphoreType.DMA((5,))],
        compiler_params=pltpu.CompilerParams(vmem_limit_bytes=16 * 1024 * 1024),
    )(*out)
    return (
        out[0].reshape(power.shape),
        out[1].reshape(units // n),
        out[2].reshape(flow.shape),
        out[3].reshape(upper.shape),
        out[4].reshape(lower.shape),
    )


def on_device(
    power,
    capacity,
    flow_dual,
    upper_dual,
    lower_dual,
    price,
    load,
    shift_factors,
    line_limit,
    unit_bus,
    leakage,
    initial_state,
    power_limit,
    capacity_cost,
):
    n = lax.axis_size("hour")
    scen, hdev, units = power.shape
    lines, buses = shift_factors.shape
    ud, rows = units // n, scen * hdev
    block = pltpu.VMEM((n, rows, ud), jnp.float32)
    vmem = pl.BlockSpec(memory_space=pltpu.VMEM)
    hbm = pl.BlockSpec(memory_space=pltpu.HBM)
    args = (
        power,
        capacity.reshape(1, ud),
        flow_dual,
        upper_dual,
        lower_dual,
        price.T,
        load.transpose(1, 0, 2),
        shift_factors,
        line_limit.reshape(1, lines),
        unit_bus.reshape(1, units),
        leakage.reshape(n, ud),
        initial_state.reshape(n, ud),
        power_limit.reshape(n, ud),
        capacity_cost.reshape(n, ud),
    )
    if scen == n and hdev == 1 and ud == 128 and lines % 1024 == 0 and buses % 128 == 0:
        return by_rows(n, args)
    results = tuple(
        jax.ShapeDtypeStruct(args[i].shape, jnp.float32) for i in range(5)
    )
    out = pl.pallas_call(
        functools.partial(kernel, n),
        out_shape=results,
        in_specs=[hbm] * 14,
        out_specs=(vmem,) * 5,
        scratch_shapes=[pltpu.VMEM(a.shape, a.dtype) for a in args]
        + [
            pltpu.VMEM((buses, units), jnp.bfloat16),
            block,
            block,
            pltpu.VMEM((rows, lines), jnp.float32),
            pltpu.VMEM((rows, units), jnp.bfloat16),
        ]
        + [block] * 8
        + [
            pltpu.SemaphoreType.DMA((4, n)),
            pltpu.SemaphoreType.DMA((4, n)),
            pltpu.SemaphoreType.DMA((14,)),
        ],
        compiler_params=pltpu.CompilerParams(
            collective_id=0, has_side_effects=True, vmem_limit_bytes=48 * 1024 * 1024
        ),
    )(*(pltpu.with_memory_space_constraint(a, pltpu.HBM) for a in args))
    out = pl.pallas_call(
        store,
        out_shape=results,
        in_specs=[vmem] * 5,
        out_specs=(hbm,) * 5,
        scratch_shapes=[pltpu.SemaphoreType.DMA((5,))],
        compiler_params=pltpu.CompilerParams(vmem_limit_bytes=16 * 1024 * 1024),
    )(*out)
    return (out[0], out[1].reshape(ud), out[2], out[3], out[4])


def solution(mesh):
    return jax.shard_map(
        on_device,
        mesh=mesh,
        in_specs=(
            P("groups", "hour", None),
            P(("groups", "hour")),
            P("groups", "hour", None),
            P("groups", "hour", None),
            P("groups", "hour", None),
            P("groups", "hour"),
            P("groups", "hour", None),
            P(),
            P(),
            P(),
            P(),
            P("groups"),
            P(),
            P(),
        ),
        out_specs=(
            P("groups", "hour", None),
            P(("groups", "hour")),
            P("groups", "hour", None),
            P("groups", "hour", None),
            P("groups", "hour", None),
        ),
        check_vma=False,
    )
```
